256 devices in a mesh: bx: 4 (over y_hi, core), by: 8 (over y_lo, x), bz: 8 (over z).
Axes of the slice: x: 4, y: 4 (y_hi: 2, y_lo: 2; y = y_hi * 2 + y_lo), z: 8, core: 2. Of those that a mesh axis runs over, the one named last changes fastest.
Arguments:
- space_factor: float32 [64, 8, 64, 1024], P(None, 'bx', 'by', 'bz'), may hold values from -6 to 6
- core_matrix: float32 [64, 64], replicated, may hold values from -0.1 to 3
- velocity_factor: float32 [64, 32768], P(None, ('bx', 'by')), may hold values from -30 to 30
Outputs:
- new_space: float32 [64, 8, 64, 1024], P(None, 'bx', 'by', 'bz')
- new_core: float32 [64, 64], replicated
- new_velocity: float32 [64, 32768], P(None, ('bx', 'by'))
The draws below stay inside these ranges and needn't reach their ends.
All inputs are finite; a program needn't handle non-finite values.
Results may differ from the reference program's by a relative error of at most 0.0028.
Values sent between devices are 32-bit elements; how exact they have to be, the bound alone decides.
No kernel may reach another device: no remote copies, remote signals or barrier semaphores. Data moves between devices by JAX's collectives and lax.ppermute only.
A program may use at most 64 MiB of HBM per device.

```python
import jax
import jax.numpy as jnp
from jax import lax

RANK = 64
VEL_N = 32
STEPS = 2
NX = 8
NY = 64
NZ = 1024
NCELLS = 524288
NVEL = 32768


def draw_core_matrix(key, part):
    key_diag, key_off = jax.random.split(key)
    diagonal = jax.random.uniform(key_diag, (RANK,), jnp.float32, 1.0, 3.0)
    off_part = jnp.clip(0.05 * jax.random.normal(key_off, (RANK, RANK), jnp.float32), -0.1, 0.1)
    mask_off = 1.0 - jnp.eye(RANK, dtype=jnp.float32)
    return jnp.diag(diagonal) + mask_off * off_part


def draw_velocity_factor(key, part):
    key_noise, key_amp, key_tilt, key_drift = jax.random.split(key, 4)
    row_ids = jnp.arange(VEL_N ** 3, dtype=jnp.int32)
    levels = jnp.stack([row_ids // (VEL_N * VEL_N), row_ids // VEL_N % VEL_N, row_ids % VEL_N]).astype(jnp.float32)
    speeds = 3.0 * (2.0 * levels + 1.0 - VEL_N) / VEL_N
    bump_shape = jnp.exp(-0.5 * jnp.sum(speeds * speeds, axis=0))
    noise_part = jnp.clip(jax.random.normal(key_noise, (RANK, VEL_N ** 3), jnp.float32), -4.0, 4.0)
    amplitude = jnp.clip(jax.random.normal(key_amp, (RANK, 1), jnp.float32), -2.0, 2.0)
    tilt_coeff = jnp.clip(3.0 * jax.random.normal(key_tilt, (RANK, 3), jnp.float32), -3.0, 3.0)
    drift_coeff = jnp.clip(jax.random.normal(key_drift, (RANK, 4), jnp.float32), -2.0, 2.0)
    tilted = tilt_coeff[:, 0:1] * speeds[0][None] + tilt_coeff[:, 1:2] * speeds[1][None] + tilt_coeff[:, 2:3] * speeds[2][None]
    drifted = drift_coeff[:, 0:1] + drift_coeff[:, 1:2] * speeds[0][None] + drift_coeff[:, 2:3] * speeds[1][None] + drift_coeff[:, 3:4] * speeds[2][None]
    return noise_part + bump_shape[None] * (4.0 * amplitude + 3.0 * tilted) + 0.3 * drifted


def steps_of(rng, extent, pieces, low, largest):
    level, own = 1.0, jax.random.fold_in(rng, 6)
    for position, parts in pieces:
        heights = jnp.exp(jax.random.uniform(jax.random.fold_in(own, position), (parts,), jnp.float32, low / len(pieces), largest / len(pieces)))
        level = level * jnp.repeat(heights, extent[position] // parts).reshape([-1 if axis == position else 1 for axis in range(len(extent))])
    return level


def gaussian(key, extent, spread, reach, shards=(), held_as=jnp.bfloat16):
    gain = steps_of(key, extent, shards, -0.22, 0.18) if shards else 1.0
    values = jax.random.normal(key, extent, jnp.float32) * spread * gain
    return jnp.minimum(jnp.maximum(values, -reach), reach).astype(held_as)


def setup_inputs(seed: int = 0) -> dict:
    key_of = jax.random.split(jax.random.key(seed), 4)
    return {
        "space_factor": gaussian(key_of[0], (RANK, NX, NY, NZ), 1.0, 6.0, ((1, 4), (2, 8), (3, 8)), jnp.float32),
        "core_matrix": draw_core_matrix(jax.random.fold_in(key_of[3], 71), 0),
        "velocity_factor": draw_velocity_factor(jax.random.fold_in(key_of[3], 71), 0),
    }


TIME_STEP = 0.1
RELAX_RATE = 1.0
SPEED_MAX = 3.0
HIGHEST = lax.Precision.HIGHEST

def matmul_hi(left_mat, right_mat):
    return jnp.dot(left_mat, right_mat, precision=HIGHEST)

def apply_left(matrix, field):
    return jnp.einsum('lj,lxyz->jxyz', matrix, field, precision=HIGHEST)

def contract(left_field, right_field):
    return lax.dot_general(left_field, right_field, (((1, 2, 3), (1, 2, 3)), ((), ())), precision=HIGHEST)

def velocity_tables(start, row_count):
    row_ids = start + jnp.arange(row_count, dtype=jnp.int32)
    levels = jnp.stack([row_ids // (VEL_N * VEL_N), row_ids // VEL_N % VEL_N, row_ids % VEL_N]).astype(jnp.float32)
    speeds = SPEED_MAX * (2.0 * levels + 1.0 - VEL_N) / VEL_N
    line_speeds = SPEED_MAX * (2.0 * jnp.arange(VEL_N, dtype=jnp.float32) + 1.0 - VEL_N) / VEL_N
    norm_one = jnp.mean(jnp.exp(-0.5 * line_speeds * line_speeds))
    weight = jnp.exp(-0.5 * jnp.sum(speeds * speeds, axis=0)) / (norm_one * norm_one * norm_one)
    eq_modes = jnp.stack([weight, weight * speeds[0], weight * speeds[1], weight * speeds[2], 0.5 * weight * (speeds[0] * speeds[0] - 1.0), 0.5 * weight * (speeds[1] * speeds[1] - 1.0), 0.5 * weight * (speeds[2] * speeds[2] - 1.0), weight * speeds[0] * speeds[1], weight * speeds[0] * speeds[2], weight * speeds[1] * speeds[2]])
    moment_rows = jnp.concatenate([jnp.ones_like(speeds[:1]), speeds], axis=0)
    return (speeds, eq_modes, moment_rows)

def quadratic(density):
    return jnp.stack([density[0], density[1], density[2], density[3], density[1] * density[1], density[2] * density[2], density[3] * density[3], density[1] * density[2], density[1] * density[3], density[2] * density[3]])

def orthonormal(raw_rows, row_total):
    flat_rows = raw_rows.reshape(raw_rows.shape[0], -1)
    gram_mat = matmul_hi(flat_rows, flat_rows.T) / row_total
    chol_low = jnp.linalg.cholesky(gram_mat)
    solved = jax.scipy.linalg.solve_triangular(chol_low, flat_rows, lower=True)
    return (solved.reshape(raw_rows.shape), chol_low)

def velocity_ops(v_rows, tables):
    speeds, eq_modes, moment_rows = tables
    plus_ops = jnp.einsum('dkv,jv->dkj', v_rows[None] * jnp.maximum(speeds, 0.0)[:, None], v_rows, precision=HIGHEST) / NVEL
    minus_ops = jnp.einsum('dkv,jv->dkj', v_rows[None] * jnp.minimum(speeds, 0.0)[:, None], v_rows, precision=HIGHEST) / NVEL
    moment_ops = matmul_hi(moment_rows, v_rows.T) / NVEL
    eq_proj = matmul_hi(eq_modes, v_rows.T) / NVEL
    return (plus_ops, minus_ops, moment_ops, eq_proj)

def reference(space_factor, core_matrix, velocity_factor):
    tables = velocity_tables(0, NVEL)
    speeds = tables[0]
    plus_speed = jnp.maximum(speeds, 0.0)
    minus_speed = jnp.minimum(speeds, 0.0)
    ident_mat = jnp.eye(RANK, dtype=jnp.float32)
    v_rows, chol_low = orthonormal(velocity_factor, NVEL)
    core_mat = matmul_hi(core_matrix, chol_low)
    x_basis = space_factor
    for turn_index in range(STEPS):
        plus_ops, minus_ops, moment_ops, eq_proj = velocity_ops(v_rows, tables)
        factor_k = apply_left(core_mat, x_basis)
        density = jnp.einsum('kj,jxyz->kxyz', moment_ops, factor_k, precision=HIGHEST)
        k_rate = RELAX_RATE * (jnp.einsum('mj,mxyz->jxyz', eq_proj, quadratic(density), precision=HIGHEST) - factor_k)
        for dim_index in range(3):
            below_k = jnp.roll(factor_k, 1, axis=dim_index + 1)
            above_k = jnp.roll(factor_k, -1, axis=dim_index + 1)
            k_rate = k_rate - apply_left(plus_ops[dim_index], factor_k - below_k) - apply_left(minus_ops[dim_index], above_k - factor_k)
        new_k = factor_k + TIME_STEP * k_rate
        x_basis, chol_low = orthonormal(new_k, NCELLS)
        core_mat = chol_low.T
        shifted = jnp.stack([contract(x_basis, jnp.roll(x_basis, 1, axis=dim_index + 1)) for dim_index in range(3)]) / NCELLS
        coeffs = matmul_hi(moment_ops, core_mat.T)
        features = quadratic(jnp.einsum('ki,ixyz->kxyz', coeffs, x_basis, precision=HIGHEST))
        moments = contract(features, x_basis) / NCELLS
        s_rate = RELAX_RATE * (matmul_hi(moments.T, eq_proj) - core_mat)
        for dim_index in range(3):
            s_rate = s_rate - matmul_hi(matmul_hi(ident_mat - shifted[dim_index], core_mat), plus_ops[dim_index])
            s_rate = s_rate - matmul_hi(matmul_hi(shifted[dim_index].T - ident_mat, core_mat), minus_ops[dim_index])
        core_mat = core_mat - TIME_STEP * s_rate
        l_factor = matmul_hi(core_mat, v_rows)
        coeffs = matmul_hi(moment_ops, core_mat.T)
        features = quadratic(jnp.einsum('ki,ixyz->kxyz', coeffs, x_basis, precision=HIGHEST))
        collide = contract(features, x_basis) / NCELLS
        l_rate = RELAX_RATE * (matmul_hi(collide.T, tables[1]) - l_factor)
        for dim_index in range(3):
            l_rate = l_rate - matmul_hi(ident_mat - shifted[dim_index], l_factor) * plus_speed[dim_index]
            l_rate = l_rate - matmul_hi(shifted[dim_index].T - ident_mat, l_factor) * minus_speed[dim_index]
        l_factor = l_factor + TIME_STEP * l_rate
        v_rows, chol_low = orthonormal(l_factor, NVEL)
        core_mat = chol_low
    return (x_basis, core_mat, v_rows)
```

```python
import jax
import jax.numpy as jnp
import numpy as np
from jax import lax
from jax.sharding import PartitionSpec as P

VEL_N = 32
STEPS = 2
TIME_STEP = 0.1
SPEED_MAX = 3.0
HIGHEST = lax.Precision.HIGHEST
PLANE = ("bx", "by")


def mm(a, b):
    return jnp.dot(a, b, precision=HIGHEST)


def mmt(a, b):
    return lax.dot_general(a, b, (((1,), (1,)), ((), ())), precision=HIGHEST)


def velocity_tables(start, row_count, xp=jnp):
    row_ids = start + xp.arange(row_count, dtype=xp.int32)
    levels = xp.stack(
        [row_ids // (VEL_N * VEL_N), row_ids // VEL_N % VEL_N, row_ids % VEL_N]
    ).astype(xp.float32)
    speeds = SPEED_MAX * (2.0 * levels + 1.0 - VEL_N) / VEL_N
    line = SPEED_MAX * (2.0 * xp.arange(VEL_N, dtype=xp.float32) + 1.0 - VEL_N) / VEL_N
    norm_one = xp.mean(xp.exp(-0.5 * line * line))
    weight = xp.exp(-0.5 * xp.sum(speeds * speeds, axis=0)) / (norm_one * norm_one * norm_one)
    modes = xp.stack(
        [
            weight,
            weight * speeds[0],
            weight * speeds[1],
            weight * speeds[2],
            0.5 * weight * (speeds[0] * speeds[0] - 1.0),
            0.5 * weight * (speeds[1] * speeds[1] - 1.0),
            0.5 * weight * (speeds[2] * speeds[2] - 1.0),
            weight * speeds[0] * speeds[1],
            weight * speeds[0] * speeds[2],
            weight * speeds[1] * speeds[2],
        ]
    )
    moment_rows = xp.concatenate([xp.ones_like(speeds[:1]), speeds], axis=0)
    return (speeds, modes, moment_rows)


def face_weights(speeds, xp=jnp):
    rows = [xp.ones_like(speeds[0])]
    for d in range(3):
        rows += [xp.maximum(speeds[d], 0.0), xp.minimum(speeds[d], 0.0)]
    return xp.stack(rows)


def grid_constants(row_total):
    speeds, modes, moments = velocity_tables(0, row_total, np)
    modes = modes.astype(np.float64)
    weights = face_weights(speeds, np).astype(np.float64)
    mode_gram = np.einsum("wv,mv,nv->wmn", weights, modes, modes)
    return mode_gram.astype(np.float32), (moments.astype(np.float64) @ modes.T).astype(np.float32)


def quadratic(d):
    return jnp.concatenate(
        [d, d[1:4] * d[1:4], d[1:2] * d[2:3], d[1:2] * d[3:4], d[2:3] * d[3:4]], axis=0
    )


def route(axis, step):
    n = lax.axis_size(axis)
    return [(i, (i + step) % n) for i in range(n)]


def swap(chunks, axis):
    return lax.all_to_all(chunks, axis, 0, 0, tiled=True)


def total(payload, over_z):
    n = lax.axis_size(PLANE)
    rows = payload.shape[0] // n
    part = jnp.sum(swap(payload.reshape(n, rows, 128), PLANE), axis=0)
    if over_z:
        nz = lax.axis_size("bz")
        part = jnp.sum(swap(jnp.broadcast_to(part[None], (nz, rows, 128)), "bz"), axis=0)
    return swap(jnp.broadcast_to(part[None], (n, rows, 128)), PLANE).reshape(n * rows, 128)


def pack(mats, rows):
    flat = jnp.concatenate(mats, axis=0)
    pad = 2 * rows - flat.shape[0]
    flat = jnp.concatenate([flat, jnp.zeros((pad, 64), jnp.float32)], axis=0)
    return jnp.concatenate([flat[:rows], flat[rows:]], axis=1)


def unpack(payload, counts):
    flat = jnp.concatenate([payload[:, :64], payload[:, 64:]], axis=0)
    out, at = [], 0
    for c in counts:
        out.append(flat[at : at + c])
        at += c
    return out


def planes(field):
    low = (
        lax.ppermute(field[:, -1:], "bx", route("bx", 1)),
        lax.ppermute(field[:, :, -1:], "by", route("by", 1)),
        lax.ppermute(field[:, :, :, -1:], "bz", route("bz", 1)),
    )
    high = (
        lax.ppermute(field[:, :1], "bx", route("bx", -1)),
        lax.ppermute(field[:, :, :1], "by", route("by", -1)),
        lax.ppermute(field[:, :, :, :1], "bz", route("bz", -1)),
    )
    return low, high


def below(field, plane, d):
    n = field.shape[d + 1]
    return jnp.concatenate([plane, lax.slice_in_dim(field, 0, n - 1, axis=d + 1)], axis=d + 1)


def above(field, plane, d):
    n = field.shape[d + 1]
    return jnp.concatenate([lax.slice_in_dim(field, 1, n, axis=d + 1), plane], axis=d + 1)


def flat(field):
    return field.reshape(field.shape[0], -1)


def chol_inverse(gram):
    low = jnp.linalg.cholesky(gram)
    inv = jax.scipy.linalg.solve_triangular(low, jnp.eye(gram.shape[0], dtype=gram.dtype), lower=True)
    return low, inv


def weighted(rows_l, modes, weights, moments):
    stack = (rows_l[None] * weights[:, None, :]).reshape(-1, rows_l.shape[1])
    quads = mmt(stack, rows_l)
    mode_stack = (modes[None] * weights[:, None, :]).reshape(-1, rows_l.shape[1])
    return quads, mmt(mode_stack, rows_l), mmt(moments, rows_l)


def operators(grams, modes_raw, moments_raw, count):
    low, inv = chol_inverse(grams[0] / count)
    side = mm(inv, grams[1:].transpose(1, 0, 2).reshape(64, -1)).reshape(64, 6, 64)
    ops = mmt(side.reshape(-1, 64), inv).reshape(64, 6, 64).transpose(1, 0, 2) / count
    return low, inv, ops, mmt(moments_raw, inv) / count, mmt(modes_raw, inv) / count


def local(space_factor, core_matrix, velocity_factor):
    rows = velocity_factor.shape[1]
    n_plane = lax.axis_size(PLANE)
    vel_count = rows * n_plane
    nz = lax.axis_size("bz")
    speeds, modes, moments = velocity_tables(lax.axis_index(PLANE) * rows, rows)
    weights = face_weights(speeds)
    mode_gram, moment_mode = grid_constants(vel_count)
    ident = jnp.eye(64, dtype=jnp.float32)
    shape = space_factor.shape
    cells = shape[1] * shape[2] * shape[3] * lax.axis_size("bx") * lax.axis_size("by") * nz

    field = space_factor
    low, high = planes(field)
    quads, mode_rows, moment_sums = weighted(velocity_factor, modes, weights, moments)
    sums = total(pack([quads, mode_rows[:10], moment_sums], 256), False)
    quads, mode_rows, moment_sums = unpack(sums, (448, 10, 4))
    c_vel, c_vel_inv, ops, mu, proj = operators(
        quads.reshape(7, 64, 64), mode_rows, moment_sums, vel_count
    )
    rows_l = velocity_factor
    turn_map = mm(core_matrix, c_vel).T
    for turn in range(STEPS):
        rows_v = mm(c_vel_inv, rows_l)
        plus, minus = ops[0::2], ops[1::2]
        stay = (1.0 - TIME_STEP) * ident + TIME_STEP * jnp.sum(minus - plus, axis=0)
        maps = [mm(stay, turn_map)]
        maps += [mm(TIME_STEP * plus[d], turn_map) for d in range(3)]
        maps += [mm(-TIME_STEP * minus[d], turn_map) for d in range(3)]
        feats = quadratic(mm(mm(mu, turn_map), flat(field)))
        parts = [flat(field)]
        parts += [flat(below(field, low[d], d)) for d in range(3)]
        parts += [flat(above(field, high[d], d)) for d in range(3)]
        new_k = mm(
            jnp.concatenate(maps + [TIME_STEP * proj.T], axis=1),
            jnp.concatenate(parts + [feats], axis=0),
        )
        field = new_k.reshape(shape)
        low, high = planes(field)
        feats = quadratic(mm(mu, new_k))
        right = [new_k] + [flat(below(field, low[d], d)) for d in range(3)] + [feats]
        sums = total(pack([mmt(jnp.concatenate(right, axis=0), new_k)], 256), True) / cells
        gram, shifts, moment_x = unpack(sums, (64, 192, 10))
        c_x, c_x_inv = chol_inverse(gram)
        sh_t = [mmt(mm(c_x_inv, shifts[64 * d : 64 * d + 64]), c_x_inv) for d in range(3)]
        moment_x = mmt(moment_x, c_x_inv)
        core = c_x.T
        rate = mm(moment_x.T, proj) - core
        for d in range(3):
            rate = rate - mm(mm(ident - sh_t[d].T, core), plus[d])
            rate = rate - mm(mm(sh_t[d] - ident, core), minus[d])
        core = core - TIME_STEP * rate
        coeffs = mmt(mu, core)
        feats = quadratic(mm(mm(coeffs, c_x_inv), new_k))
        collide = mmt(feats, new_k)
        sv = mm(core, rows_v)
        steps = [(1.0 - TIME_STEP) * ident]
        for d in range(3):
            steps += [-TIME_STEP * (ident - sh_t[d].T), -TIME_STEP * (sh_t[d] - ident)]
        sv_stack = (sv[None] * weights[:, None, :]).reshape(-1, rows)
        rows_a = mm(jnp.concatenate(steps, axis=1), sv_stack)
        last = turn + 1 == STEPS
        if last:
            quads, mode_rows = mmt(rows_a, rows_a), mmt(modes, rows_a)
            mats = [quads / nz, mode_rows / nz, collide]
            quads, mode_rows, collide = unpack(total(pack(mats, 256), True), (64, 10, 10))
        else:
            quads, mode_rows, moment_sums = weighted(rows_a, modes, weights, moments)
            mats = [quads / nz, mode_rows / nz, moment_sums / nz, collide]
            quads, mode_rows, moment_sums, collide = unpack(
                total(pack(mats, 512), True), (448, 70, 4, 10)
            )
        gain = TIME_STEP * mmt(collide / cells, c_x_inv).T
        rows_l = rows_a + mm(gain, modes)
        if last:
            cross = mm(gain, mode_rows)
            grams = quads + cross + cross.T + mm(gain, mmt(mode_gram[0], gain))
            c_vel, c_vel_inv = chol_inverse(grams / vel_count)
            return (mm(c_x_inv, new_k).reshape(shape), c_vel, mm(c_vel_inv, rows_l))
        mode_rows = mode_rows.reshape(7, 10, 64)
        grams = []
        for w in range(7):
            cross = mm(gain, mode_rows[w])
            grams.append(quads[64 * w : 64 * w + 64] + cross + cross.T + mm(gain, mmt(mode_gram[w], gain)))
        c_vel, c_vel_inv, ops, mu, proj = operators(
            jnp.stack(grams),
            mode_rows[0] + mmt(mode_gram[0], gain),
            moment_sums + mmt(moment_mode, gain),
            vel_count,
        )
        turn_map = mm(c_vel.T, c_x_inv)


def solution(mesh):
    return jax.shard_map(
        local,
        mesh=mesh,
        in_specs=(P(None, "bx", "by", "bz"), P(), P(None, PLANE)),
        out_specs=(P(None, "bx", "by", "bz"), P(), P(None, PLANE)),
        check_vma=False,
    )
```

```python
import functools

import jax
import jax.numpy as jnp
import numpy as np
from jax import lax
from jax.experimental import pallas as pl
from jax.experimental.pallas import tpu as pltpu
from jax.sharding import PartitionSpec as P

VEL_N = 32
STEPS = 2
TIME_STEP = 0.1
SPEED_MAX = 3.0
HIGHEST = lax.Precision.HIGHEST
PLANE = ("bx", "by")
RANK = 64
F32 = jnp.float32


def mm(a, b):
    return jnp.dot(a, b, precision=HIGHEST, preferred_element_type=F32)


def mmt(a, b):
    return lax.dot_general(
        a, b, (((1,), (1,)), ((), ())), precision=HIGHEST, preferred_element_type=F32
    )


def np_tables(row_total):
    row_ids = np.arange(row_total)
    levels = np.stack([row_ids // (VEL_N * VEL_N), row_ids // VEL_N % VEL_N, row_ids % VEL_N])
    v = SPEED_MAX * (2.0 * levels + 1.0 - VEL_N) / VEL_N
    w = np.exp(-0.5 * np.sum(v * v, axis=0)) / line_mean() ** 3
    modes = np.stack(
        [w, w * v[0], w * v[1], w * v[2]]
        + [0.5 * w * (v[d] * v[d] - 1.0) for d in range(3)]
        + [w * v[0] * v[1], w * v[0] * v[2], w * v[1] * v[2]]
    )
    weights = [np.ones_like(w)]
    for d in range(3):
        weights += [np.maximum(v[d], 0.0), np.minimum(v[d], 0.0)]
    return v, modes, np.stack(weights)


def line_mean():
    line = SPEED_MAX * (2.0 * np.arange(VEL_N) + 1.0 - VEL_N) / VEL_N
    return float(np.mean(np.exp(-0.5 * line * line)))


def constants(row_total):
    v, modes, weights = np_tables(row_total)
    gram = np.einsum("wv,mv,nv->wmn", weights, modes, modes)
    out = np.zeros((160, 16), np.float32)
    for w in range(7):
        out[16 * w : 16 * w + 10, :10] = gram[w]
    out[112, :10] = modes.sum(axis=1)
    for d in range(3):
        out[113 + d, :10] = modes @ v[d]
    first = [0, 1, 2, 3, 1, 2, 3, 1, 1, 2]
    second = [None, None, None, None, 1, 2, 3, 2, 3, 3]
    for r in range(10):
        out[120 + r, first[r]] = 1.0
        if second[r] is not None:
            out[136 + r, second[r]] = 1.0
    return out


def iota(shape, dim):
    return lax.broadcasted_iota(jnp.int32, shape, dim)


def eye():
    return (iota((RANK, RANK), 0) == iota((RANK, RANK), 1)).astype(F32)


def chol_inverse(gram):
    lane = iota((8, 128), 1)
    sub = iota((8, 128), 0)
    wide = jnp.concatenate([gram, jnp.zeros_like(gram)], axis=1)
    blocks = []
    for b in range(8):
        unit = jnp.where(lane == sub + (64 + 8 * b), 1.0, 0.0)
        blocks.append(wide[8 * b : 8 * b + 8] + unit)
    for k in range(RANK):
        b, r = divmod(k, 8)
        head = blocks[b]
        scale = lax.rsqrt(jnp.broadcast_to(head[r : r + 1, k : k + 1], (8, 128)))
        row = jnp.broadcast_to(head[r : r + 1, :], (8, 128)) * scale
        for i in range(b, 8):
            blk = blocks[i]
            col = jnp.broadcast_to(blk[:, k : k + 1], (8, 128)) * scale
            new = blk - col * row
            if i == b:
                new = jnp.where(sub > r, new, jnp.where(sub == r, row, blk))
            blocks[i] = new
    full = jnp.concatenate(blocks, axis=0)
    keep = iota((RANK, RANK), 1) >= iota((RANK, RANK), 0)
    return jnp.where(keep, full[:, :RANK], 0.0), full[:, RANK:]


def features(sel_map, field):
    both = mm(sel_map, field)
    lift = jnp.where(iota((16, field.shape[1]), 0) < 4, 1.0, 0.0)
    return both[:16] * (both[16:] + lift)


def pair_block(plus, minus):
    return jnp.where(iota((RANK, RANK), 0) <= iota((RANK, RANK), 1), plus, minus)


def weighted_payload(rows, v1, tab_ref, out_ref, stack_ref, scale, collide, full):
    modes = tab_ref[0:16, :]
    v2, v3 = tab_ref[18:19, :], tab_ref[19:20, :]
    weights = [None, jnp.maximum(v2, 0.0), jnp.minimum(v2, 0.0)]
    weights += [jnp.maximum(v3, 0.0), jnp.minimum(v3, 0.0)]
    count = 5 if full else 1
    for i in range(count):
        w = weights[i]
        stack_ref[80 * i : 80 * i + 64, :] = rows if w is None else rows * w
        stack_ref[80 * i + 64 : 80 * i + 80, :] = modes if w is None else modes * w
    if full:
        stack_ref[400:408, :] = tab_ref[16:24, :]
        res = mmt(stack_ref[...], rows) * scale
    else:
        res = mmt(stack_ref[0:80, :], rows) * scale
    quads = [res[80 * i : 80 * i + 64] for i in range(count)]
    cross = [res[80 * i + 64 : 80 * i + 80] for i in range(count)]
    out_ref[...] = jnp.zeros_like(out_ref)
    out_ref[0:64, 0:64] = quads[0]
    out_ref[128:144, 0:64] = cross[0]
    if collide is not None:
        out_ref[136:152, 64:128] = collide
    if full:
        v1p, v1m = jnp.maximum(v1, 0.0), jnp.minimum(v1, 0.0)
        pairs = [(quads[0] * v1p, quads[0] * v1m), (quads[1], quads[2]), (quads[3], quads[4])]
        crosses = [cross[0] * v1p, cross[0] * v1m] + cross[1:]
        out_ref[0:64, 64:128] = pair_block(*pairs[1])
        out_ref[64:128, 0:64] = pair_block(*pairs[0])
        out_ref[64:128, 64:128] = pair_block(*pairs[2])
        for i in range(6):
            out_ref[144 + 16 * i : 160 + 16 * i, 0:64] = crosses[i]
        out_ref[128:136, 64:128] = res[400:408]
        for d in range(3):
            diag = jnp.sum(pairs[d][1] * eye(), axis=0, keepdims=True)
            out_ref[152 + d : 153 + d, 64:128] = diag


def start_kernel(v1_ref, rows_ref, out_ref, tab_ref, stack_ref):
    v1 = v1_ref[0, 0]
    lanes = tab_ref.shape[1]
    at = iota((1, lanes), 1)
    v2 = SPEED_MAX * (2.0 * (at // VEL_N).astype(F32) + 1.0 - VEL_N) / VEL_N
    v3 = SPEED_MAX * (2.0 * (at % VEL_N).astype(F32) + 1.0 - VEL_N) / VEL_N
    v1 = jnp.full((1, lanes), v1, F32)
    w = jnp.exp(-0.5 * (v1 * v1 + v2 * v2 + v3 * v3)) / (line_mean() ** 3)
    tab_ref[...] = jnp.zeros_like(tab_ref)
    modes = [w, w * v1, w * v2, w * v3]
    modes += [0.5 * w * (v * v - 1.0) for v in (v1, v2, v3)]
    modes += [w * v1 * v2, w * v1 * v3, w * v2 * v3]
    for i, m in enumerate(modes):
        tab_ref[i : i + 1, :] = m
    for i, m in enumerate([jnp.ones_like(v1), v1, v2, v3]):
        tab_ref[16 + i : 17 + i, :] = m
    weighted_payload(rows_ref[...], v1_ref[0, 0], tab_ref, out_ref, stack_ref, 1.0, None, True)


def symmetric(sums, gain, cons):
    upper = iota((RANK, RANK), 0) <= iota((RANK, RANK), 1)
    diag = iota((RANK, RANK), 0) == iota((RANK, RANK), 1)
    packs = [sums[64:128, 0:64], sums[0:64, 64:128], sums[64:128, 64:128]]
    grams = [sums[0:64, 0:64]]
    for d in range(3):
        turned = packs[d].T
        grams.append(jnp.where(upper, packs[d], turned))
        grams.append(
            jnp.where(diag, sums[152 + d : 153 + d, 64:128], jnp.where(upper, turned, packs[d]))
        )
    mode_rows, moments = sums[128:144, 0:64], sums[128:136, 64:128]
    if gain is not None:
        mode_gain = mmt(cons[0:120], gain)
        for w in range(7):
            half = sums[128 + 16 * w : 144 + 16 * w, 0:64] + 0.5 * mode_gain[16 * w : 16 * w + 16]
            cross = mm(gain, half)
            grams[w] = grams[w] + (cross + cross.T)
        mode_rows = mode_rows + mode_gain[0:16]
        moments = moments + mode_gain[112:120]
    return grams, mode_rows, moments


def shifted_stack(p, stack_ref, mine, lower, upper, yl_ref, yh_ref, zl_ref, zh_ref):
    lane = iota((RANK, 128), 1)
    field = mine[...]
    stack_ref[0:64, :] = field
    stack_ref[64:128, :] = lower[...]
    stack_ref[256:320, :] = upper[...]
    n = field.shape[1] // 128
    zl, zh = zl_ref[...], zh_ref[...]
    for y in range(n):
        here = field[:, 128 * y : 128 * y + 128]
        cols = slice(128 * y, 128 * y + 128)
        halo = slice(128 * p, 128 * p + 128)
        stack_ref[128:192, cols] = yl_ref[:, halo] if y == 0 else field[:, 128 * (y - 1) : 128 * y]
        stack_ref[320:384, cols] = (
            yh_ref[:, halo] if y == n - 1 else field[:, 128 * (y + 1) : 128 * (y + 2)]
        )
        g = p * n + y
        low = pltpu.roll(zl, (128 - g) % 128, 1)
        stack_ref[192:256, cols] = jnp.where(lane == 0, low, pltpu.roll(here, 1, 1))
        high = pltpu.roll(zh, 127 - g, 1)
        stack_ref[384:448, cols] = jnp.where(lane == 127, high, pltpu.roll(here, 127, 1))


def maps_kernel(
    first, count, cells, sums_ref, base_ref, cons_ref, fa, fb, xh, yl, yh, zl, zh,
    kb_ref, map_ref, sel_ref, seln_ref, gw_ref, mode_ref, mom_ref, civ_ref, ginv_ref, gain_ref,
    stack_ref,
):
    sums, base, cons = sums_ref[...], base_ref[...], cons_ref[...]
    gain = None
    if not first:
        gain = (TIME_STEP / cells) * mmt(base, sums[136:152, 64:128])
        gain_ref[...] = gain
    else:
        gain_ref[...] = jnp.zeros_like(gain_ref)
    grams, mode_rows, moments = symmetric(sums, gain, cons)
    shifted_stack(1, stack_ref, fb, fa, xh, yl, yh, zl, zh)
    times = mmt if first else mm
    sides = times(jnp.concatenate(grams, axis=0), base)
    sides = [sides[64 * w : 64 * w + 64] for w in range(7)]
    stay = (1.0 - TIME_STEP) * sides[0]
    for d in range(3):
        stay = stay + TIME_STEP * (sides[2 * d + 2] - sides[2 * d + 1])
    row = [stay] + [TIME_STEP * sides[2 * d + 1] for d in range(3)]
    row += [-TIME_STEP * sides[2 * d + 2] for d in range(3)] + [TIME_STEP * mode_rows.T]
    row = jnp.concatenate(row, axis=1) * (1.0 / count)
    sel = mm(cons[120:152, 0:8], times(moments, base) * (1.0 / count))
    sel_ref[...] = sel
    stack_ref[448:464, :] = features(sel, fb[...])
    gw_ref[...] = jnp.concatenate(grams[1:], axis=1)
    mode_ref[...] = mode_rows
    mom_ref[...] = moments
    _, civ = chol_inverse(grams[0] * (1.0 / count))
    maps = mm(civ, row)
    kb_ref[...] = mm(maps, stack_ref[...])
    map_ref[...] = maps
    civ_ref[...] = civ
    ginv_ref[...] = mm(civ.T, civ) * (1.0 / count)
    seln_ref[...] = mm(cons[120:152, 0:8], mmt(moments, civ) * (1.0 / count))


def columns(fields, lane_at):
    lane = iota((RANK, 128), 1)
    out = jnp.zeros((RANK, 128), F32)
    g = 0
    for field in fields:
        for y in range(field.shape[1] // 128):
            here = field[:, 128 * y : 128 * y + 128]
            out = jnp.where(lane == g, pltpu.roll(here, (g - lane_at) % 128, 1), out)
            g += 1
    return out


def plane_kernel(
    map_ref, sel_ref, fa, fb, xl, yl, yh, zl, zh, kb,
    ka_ref, ylo_ref, yho_ref, zlo_ref, zho_ref, stack_ref,
):
    shifted_stack(0, stack_ref, fa, xl, fb, yl, yh, zl, zh)
    stack_ref[448:464, :] = features(sel_ref[...], fa[...])
    ka = mm(map_ref[...], stack_ref[...])
    ka_ref[...] = ka
    kb = kb[...]
    n = ka.shape[1]
    ylo_ref[...] = jnp.concatenate([ka[:, n - 128 :], kb[:, n - 128 :]], axis=1)
    yho_ref[...] = jnp.concatenate([ka[:, :128], kb[:, :128]], axis=1)
    zlo_ref[...] = columns((ka, kb), 127)
    zho_ref[...] = columns((ka, kb), 0)


def inner_kernel(seln_ref, ka, kb, out_ref, stack_ref):
    lane = iota((RANK, 128), 1)
    n = ka.shape[1]
    zero = jnp.zeros((RANK, 128), F32)
    for p, ref in enumerate((ka, kb)):
        at = p * n
        field = ref[...]
        stack_ref[0:64, at : at + n] = field
        stack_ref[128:192, at : at + 128] = zero
        stack_ref[128:192, at + 128 : at + n] = field[:, : n - 128]
        for y in range(n // 128):
            here = field[:, 128 * y : 128 * y + 128]
            stack_ref[192:256, at + 128 * y : at + 128 * y + 128] = jnp.where(
                lane == 0, 0.0, pltpu.roll(here, 1, 1)
            )
        stack_ref[256:272, at : at + n] = features(seln_ref[...], field)
    stack_ref[64:128, 0:n] = jnp.zeros((RANK, n), F32)
    stack_ref[64:128, n : 2 * n] = ka[...]
    out_ref[...] = mmt(stack_ref[...], stack_ref[0:64, :])


def edge_kernel(part_ref, ka, xl, yl, yh, zl, zh, out_ref):
    part = part_ref[...]
    out_ref[...] = jnp.zeros_like(out_ref)
    out_ref[0:64, 0:64] = part[0:64]
    out_ref[0:64, 64:128] = part[64:128] + mmt(xl[...], ka[...])
    out_ref[64:128, 0:64] = part[128:192] + mmt(yl[...], yh[...])
    out_ref[64:128, 64:128] = part[192:256] + mmt(zl[...], zh[...])
    out_ref[128:144, 0:64] = part[256:272]


def core_kernel(
    first, last, count, cells, nz, v1_ref, sums_ref, ka, kb, rows_ref, gain_ref, tab_ref, cons_ref,
    gw_ref, mode_ref, mom_ref, civ_ref, ginv_ref, out_ref, rows_out, cxi_ref, stack_ref,
):
    v1 = v1_ref[0, 0]
    sums = sums_ref[...] * (1.0 / cells)
    civ = civ_ref[...]
    unit = eye()
    up, cxi = chol_inverse(sums[0:64, 0:64])
    cxi_ref[...] = cxi
    y = mm(up, civ)
    zs = jnp.concatenate([sums[0:64, 64:128], sums[64:128, 0:64], sums[64:128, 64:128]], axis=0)
    zs = mmt(zs, cxi)
    lower, upper = [], []
    for d in range(3):
        turned = mm(cxi, zs[64 * d : 64 * d + 64])
        lower.append(unit - turned.T)
        upper.append(turned - unit)
    yg = mm(y, gw_ref[...])
    yg = jnp.concatenate([yg[:, 64 * w : 64 * w + 64] for w in range(6)], axis=0)
    sides = jnp.concatenate([lower[0], upper[0], lower[1], upper[1], lower[2], upper[2]], axis=1)
    rate = mm(mmt(cxi, sums[128:144, 0:64]), mode_ref[...]) - mm(sides, yg)
    y = (1.0 + TIME_STEP) * y - TIME_STEP * mm(rate, ginv_ref[...])
    sel = mm(cons_ref[120:152, 0:8], mm(mmt(mom_ref[...], y) * (1.0 / count), cxi))
    collide = mmt(features(sel, ka[...]), ka[...]) + mmt(features(sel, kb[...]), kb[...])
    rows = rows_ref[...]
    if not first:
        rows = rows + mm(gain_ref[...], tab_ref[0:16, :])
    sv = mm(y, rows)
    v2, v3 = tab_ref[18:19, :], tab_ref[19:20, :]
    stack_ref[0:64, :] = sv
    stack_ref[64:128, :] = sv * jnp.maximum(v2, 0.0)
    stack_ref[128:192, :] = sv * jnp.minimum(v2, 0.0)
    stack_ref[192:256, :] = sv * jnp.maximum(v3, 0.0)
    stack_ref[256:320, :] = sv * jnp.minimum(v3, 0.0)
    turn = lower[0] * jnp.maximum(v1, 0.0) + upper[0] * jnp.minimum(v1, 0.0)
    move = [(1.0 - TIME_STEP) * unit - TIME_STEP * turn]
    move += [-TIME_STEP * m for m in (lower[1], upper[1], lower[2], upper[2])]
    rows = mm(jnp.concatenate(move, axis=1), stack_ref[0:320, :])
    rows_out[...] = rows
    weighted_payload(rows, v1, tab_ref, out_ref, stack_ref, 1.0 / nz, collide, not last)


def finish_kernel(count, cells, sums_ref, cxi_ref, rows_ref, tab_ref, cons_ref, low_ref, out_ref):
    sums = sums_ref[...]
    gain = (TIME_STEP / cells) * mmt(cxi_ref[...], sums[136:152, 64:128])
    half = sums[128:144, 0:64] + 0.5 * mmt(cons_ref[0:16, :], gain)
    cross = mm(gain, half)
    up, civ = chol_inverse((sums[0:64, 0:64] + (cross + cross.T)) * (1.0 / count))
    low_ref[...] = up.T
    out_ref[...] = mm(civ, rows_ref[...] + mm(gain, tab_ref[0:16, :]))


def call(kernel, outs, scratch, *args):
    shapes = [jax.ShapeDtypeStruct(s, F32) for s in outs]
    specs = [pl.BlockSpec(memory_space=pltpu.VMEM) for _ in args]
    if args[0].shape == (1, 1):
        specs[0] = pl.BlockSpec(memory_space=pltpu.SMEM)
    return pl.pallas_call(
        kernel,
        out_shape=shapes,
        in_specs=specs,
        out_specs=[pl.BlockSpec(memory_space=pltpu.VMEM) for _ in outs],
        scratch_shapes=[pltpu.VMEM(scratch, F32)] if scratch else [],
        compiler_params=pltpu.CompilerParams(vmem_limit_bytes=40 * 1024 * 1024),
    )(*args)


def route(axis, step):
    n = lax.axis_size(axis)
    return [(i, (i + step) % n) for i in range(n)]


def swap(chunks, axis):
    return lax.all_to_all(chunks, axis, 0, 0, tiled=True)


def total(payload, over_z):
    n = lax.axis_size(PLANE)
    rows = payload.shape[0] // n
    part = jnp.sum(swap(payload.reshape(n, rows, 128), PLANE), axis=0)
    if over_z:
        nz = lax.axis_size("bz")
        part = jnp.sum(swap(jnp.broadcast_to(part[None], (nz, rows, 128)), "bz"), axis=0)
    return swap(jnp.broadcast_to(part[None], (n, rows, 128)), PLANE).reshape(n * rows, 128)


def local(space_factor, core_matrix, velocity_factor):
    vel_rows = velocity_factor.shape[1]
    plane = lax.axis_index(PLANE)
    count = vel_rows * lax.axis_size(PLANE)
    nz = lax.axis_size("bz")
    shape = space_factor.shape
    half = shape[2] * shape[3]
    cells = 2 * half * lax.axis_size(PLANE) * nz
    cons = jnp.asarray(constants(count))
    digit = (plane * vel_rows) // (VEL_N * VEL_N)
    v1 = SPEED_MAX * (2.0 * digit.astype(F32) + 1.0 - VEL_N) / VEL_N
    v1 = v1.reshape(1, 1)

    fa = space_factor[:, 0].reshape(RANK, half)
    fb = space_factor[:, 1].reshape(RANK, half)
    payload, tab = call(
        start_kernel, [(256, 128), (24, vel_rows)], (408, vel_rows), v1, velocity_factor
    )
    yl = space_factor[:, :, -1].reshape(RANK, 256)
    yh = space_factor[:, :, 0].reshape(RANK, 256)
    pad = jnp.zeros((RANK, 128 - 2 * shape[2]), F32)
    zl = jnp.concatenate([space_factor[:, :, :, -1].reshape(RANK, -1), pad], axis=1)
    zh = jnp.concatenate([space_factor[:, :, :, 0].reshape(RANK, -1), pad], axis=1)

    def low_halo(xl, yl, zl):
        return (
            lax.ppermute(xl, "bx", route("bx", 1)),
            lax.ppermute(yl, "by", route("by", 1)),
            lax.ppermute(zl, "bz", route("bz", 1)),
        )

    def high_halo(xh, yh, zh):
        return (
            lax.ppermute(xh, "bx", route("bx", -1)),
            lax.ppermute(yh, "by", route("by", -1)),
            lax.ppermute(zh, "bz", route("bz", -1)),
        )

    low = low_halo(fb, yl, zl)
    high = high_halo(fa, yh, zh)
    sums = total(payload, False)
    base, rows = core_matrix, velocity_factor
    for turn in range(STEPS):
        first, last = turn == 0, turn + 1 == STEPS
        kb, maps, sel, seln, gw, mode_rows, moments, civ, ginv, gain = call(
            functools.partial(maps_kernel, first, count, cells),
            [(RANK, half), (RANK, 464), (32, RANK), (32, RANK), (RANK, 384), (16, RANK), (8, RANK),
             (RANK, RANK), (RANK, RANK), (RANK, 16)],
            (464, half),
            sums, base, cons, fa, fb, high[0], low[1], high[1], low[2], high[2],
        )
        ka, yl, yh, zl, zh = call(
            plane_kernel,
            [(RANK, half), (RANK, 256), (RANK, 256), (RANK, 128), (RANK, 128)],
            (464, half),
            maps, sel, fa, fb, low[0], low[1], high[1], low[2], high[2], kb,
        )
        low = low_halo(kb, yl, zl)
        (part,) = call(inner_kernel, [(272, RANK)], (272, 2 * half), seln, ka, kb)
        (payload,) = call(edge_kernel, [(256, 128)], None, part, ka, low[0], low[1], yh, low[2], zh)
        fa, fb = ka, kb
        if not last:
            high = high_halo(ka, yh, zh)
        sums = total(payload, True)
        payload, rows, base = call(
            functools.partial(core_kernel, first, last, count, cells, nz),
            [(256, 128), (RANK, vel_rows), (RANK, RANK)],
            (408, vel_rows),
            v1, sums, ka, kb, rows, gain, tab, cons, gw, mode_rows, moments, civ, ginv,
        )
        sums = total(payload, True)
    new_space = jnp.stack(
        [mm(base, ka).reshape(RANK, *shape[2:]), mm(base, kb).reshape(RANK, *shape[2:])], axis=1
    )
    new_core, new_velocity = call(
        functools.partial(finish_kernel, count, cells),
        [(RANK, RANK), (RANK, vel_rows)], None, sums, base, rows, tab, cons,
    )
    return new_space, new_core, new_velocity


def solution(mesh):
    return jax.shard_map(
        local,
        mesh=mesh,
        in_specs=(P(None, "bx", "by", "bz"), P(), P(None, PLANE)),
        out_specs=(P(None, "bx", "by", "bz"), P(), P(None, PLANE)),
        check_vma=False,
    )
```

```python
import functools

import jax
import jax.numpy as jnp
import numpy as np
from jax import lax
from jax.experimental import pallas as pl
from jax.experimental.pallas import tpu as pltpu
from jax.sharding import PartitionSpec as P

VEL_N = 32
STEPS = 2
TIME_STEP = 0.1
SPEED_MAX = 3.0
HIGHEST = lax.Precision.HIGHEST
PLANE = ("bx", "by")
RANK = 64
F32 = jnp.float32


def mm(a, b):
    return jnp.dot(a, b, precision=HIGHEST, preferred_element_type=F32)


def mmt(a, b):
    return lax.dot_general(
        a, b, (((1,), (1,)), ((), ())), precision=HIGHEST, preferred_element_type=F32
    )


def np_tables(row_total):
    row_ids = np.arange(row_total)
    levels = np.stack([row_ids // (VEL_N * VEL_N), row_ids // VEL_N % VEL_N, row_ids % VEL_N])
    v = SPEED_MAX * (2.0 * levels + 1.0 - VEL_N) / VEL_N
    w = np.exp(-0.5 * np.sum(v * v, axis=0)) / line_mean() ** 3
    modes = np.stack(
        [w, w * v[0], w * v[1], w * v[2]]
        + [0.5 * w * (v[d] * v[d] - 1.0) for d in range(3)]
        + [w * v[0] * v[1], w * v[0] * v[2], w * v[1] * v[2]]
    )
    weights = [np.ones_like(w)]
    for d in range(3):
        weights += [np.maximum(v[d], 0.0), np.minimum(v[d], 0.0)]
    return v, modes, np.stack(weights)


def line_mean():
    line = SPEED_MAX * (2.0 * np.arange(VEL_N) + 1.0 - VEL_N) / VEL_N
    return float(np.mean(np.exp(-0.5 * line * line)))


def constants(row_total):
    v, modes, weights = np_tables(row_total)
    gram = np.einsum("wv,mv,nv->wmn", weights, modes, modes)
    out = np.zeros((160, 16), np.float32)
    for w in range(7):
        out[16 * w : 16 * w + 10, :10] = gram[w]
    out[112, :10] = modes.sum(axis=1)
    for d in range(3):
        out[113 + d, :10] = modes @ v[d]
    first = [0, 1, 2, 3, 1, 2, 3, 1, 1, 2]
    second = [None, None, None, None, 1, 2, 3, 2, 3, 3]
    for r in range(10):
        out[120 + r, first[r]] = 1.0
        if second[r] is not None:
            out[136 + r, second[r]] = 1.0
    return out


def iota(shape, dim):
    return lax.broadcasted_iota(jnp.int32, shape, dim)


def eye():
    return (iota((RANK, RANK), 0) == iota((RANK, RANK), 1)).astype(F32)


def spread_lane(block, k):
    return jnp.broadcast_to(block[:, k : k + 1], (8, 128))


def spread_row(block, r):
    return jnp.broadcast_to(block[r : r + 1, :], (8, 128))


def chol_inverse(gram, width=4):
    lane = iota((8, 128), 1)
    sub = iota((8, 128), 0)
    on_diag = gram * eye()
    diag = jnp.sum(on_diag, axis=0, keepdims=True)
    row_scale = lax.rsqrt(diag)
    scaled = gram * row_scale * lax.rsqrt(jnp.sum(on_diag, axis=1, keepdims=True))
    wide = jnp.concatenate([scaled, jnp.zeros_like(gram)], axis=1)
    blocks = []
    for b in range(8):
        unit = jnp.where(lane == sub + (64 + 8 * b), 1.0, 0.0)
        blocks.append(wide[8 * b : 8 * b + 8] + unit)
    for k in range(0, RANK, width):
        b, r = divmod(k, 8)
        left = range(b, 8)
        cols = [{i: spread_lane(blocks[i], k + j) for i in left} for j in range(width)]
        heads = [spread_row(blocks[b], r + j) for j in range(width)]
        for j in range(0, width, 2):
            p = spread_row(cols[j][b], r + j)
            q = spread_row(cols[j][b], r + j + 1)
            s = spread_row(cols[j + 1][b], r + j + 1)
            inv_p = lax.rsqrt(p)
            both = inv_p * lax.rsqrt(p * s - q * q)
            pb, qb = both * p, both * q
            for i in left:
                first = cols[j][i]
                cols[j][i] = first * inv_p
                cols[j + 1][i] = pb * cols[j + 1][i] - qb * first
            first = heads[j]
            heads[j] = first * inv_p
            heads[j + 1] = pb * heads[j + 1] - qb * first
            for m in range(j + 2, width):
                u = spread_row(cols[j][b], r + m)
                w = spread_row(cols[j + 1][b], r + m)
                for i in left:
                    cols[m][i] = (cols[m][i] - cols[j][i] * u) - cols[j + 1][i] * w
                heads[m] = (heads[m] - heads[j] * u) - heads[j + 1] * w
        for i in left:
            if i == b and r + width == 8:
                new = blocks[i]
            else:
                new = blocks[i]
                for j in range(width):
                    new = new - cols[j][i] * heads[j]
            if i == b:
                new = jnp.where(sub >= r + width, new, blocks[i])
                for j in range(width):
                    new = jnp.where(sub == r + j, heads[j], new)
            blocks[i] = new
    full = jnp.concatenate(blocks, axis=0)
    keep = iota((RANK, RANK), 1) >= iota((RANK, RANK), 0)
    upper = jnp.where(keep, full[:, :RANK], 0.0) * (diag * row_scale)
    return upper, full[:, RANK:] * row_scale


def features(sel_map, field):
    both = mm(sel_map, field)
    lift = jnp.where(iota((16, field.shape[1]), 0) < 4, 1.0, 0.0)
    return both[:16] * (both[16:] + lift)


def pair_block(plus, minus):
    return jnp.where(iota((RANK, RANK), 0) <= iota((RANK, RANK), 1), plus, minus)


def weighted_payload(rows, v1, tab_ref, out_ref, stack_ref, scale, collide, full):
    modes = tab_ref[0:16, :]
    v2, v3 = tab_ref[18:19, :], tab_ref[19:20, :]
    weights = [None, jnp.maximum(v2, 0.0), jnp.minimum(v2, 0.0)]
    weights += [jnp.maximum(v3, 0.0), jnp.minimum(v3, 0.0)]
    count = 5 if full else 1
    for i in range(count):
        w = weights[i]
        stack_ref[80 * i : 80 * i + 64, :] = rows if w is None else rows * w
        stack_ref[80 * i + 64 : 80 * i + 80, :] = modes if w is None else modes * w
    if full:
        stack_ref[400:408, :] = tab_ref[16:24, :]
        res = mmt(stack_ref[...], rows) * scale
    else:
        res = mmt(stack_ref[0:80, :], rows) * scale
    quads = [res[80 * i : 80 * i + 64] for i in range(count)]
    cross = [res[80 * i + 64 : 80 * i + 80] for i in range(count)]
    out_ref[...] = jnp.zeros_like(out_ref)
    out_ref[0:64, 0:64] = quads[0]
    out_ref[128:144, 0:64] = cross[0]
    if collide is not None:
        out_ref[136:152, 64:128] = collide
    if full:
        v1p, v1m = jnp.maximum(v1, 0.0), jnp.minimum(v1, 0.0)
        pairs = [(quads[0] * v1p, quads[0] * v1m), (quads[1], quads[2]), (quads[3], quads[4])]
        crosses = [cross[0] * v1p, cross[0] * v1m] + cross[1:]
        out_ref[0:64, 64:128] = pair_block(*pairs[1])
        out_ref[64:128, 0:64] = pair_block(*pairs[0])
        out_ref[64:128, 64:128] = pair_block(*pairs[2])
        for i in range(6):
            out_ref[144 + 16 * i : 160 + 16 * i, 0:64] = crosses[i]
        out_ref[128:136, 64:128] = res[400:408]
        for d in range(3):
            diag = jnp.sum(pairs[d][1] * eye(), axis=0, keepdims=True)
            out_ref[152 + d : 153 + d, 64:128] = diag


def start_kernel(v1_ref, rows_ref, out_ref, tab_ref, stack_ref):
    v1 = v1_ref[0, 0]
    lanes = tab_ref.shape[1]
    at = iota((1, lanes), 1)
    v2 = SPEED_MAX * (2.0 * (at // VEL_N).astype(F32) + 1.0 - VEL_N) / VEL_N
    v3 = SPEED_MAX * (2.0 * (at % VEL_N).astype(F32) + 1.0 - VEL_N) / VEL_N
    v1 = jnp.full((1, lanes), v1, F32)
    w = jnp.exp(-0.5 * (v1 * v1 + v2 * v2 + v3 * v3)) / (line_mean() ** 3)
    tab_ref[...] = jnp.zeros_like(tab_ref)
    modes = [w, w * v1, w * v2, w * v3]
    modes += [0.5 * w * (v * v - 1.0) for v in (v1, v2, v3)]
    modes += [w * v1 * v2, w * v1 * v3, w * v2 * v3]
    for i, m in enumerate(modes):
        tab_ref[i : i + 1, :] = m
    for i, m in enumerate([jnp.ones_like(v1), v1, v2, v3]):
        tab_ref[16 + i : 17 + i, :] = m
    weighted_payload(rows_ref[...], v1_ref[0, 0], tab_ref, out_ref, stack_ref, 1.0, None, True)


def symmetric(sums, gain, cons):
    upper = iota((RANK, RANK), 0) <= iota((RANK, RANK), 1)
    diag = iota((RANK, RANK), 0) == iota((RANK, RANK), 1)
    packs = [sums[64:128, 0:64], sums[0:64, 64:128], sums[64:128, 64:128]]
    grams = [sums[0:64, 0:64]]
    for d in range(3):
        turned = packs[d].T
        grams.append(jnp.where(upper, packs[d], turned))
        grams.append(
            jnp.where(diag, sums[152 + d : 153 + d, 64:128], jnp.where(upper, turned, packs[d]))
        )
    mode_rows, moments = sums[128:144, 0:64], sums[128:136, 64:128]
    if gain is not None:
        mode_gain = mmt(cons[0:120], gain)
        for w in range(7):
            half = sums[128 + 16 * w : 144 + 16 * w, 0:64] + 0.5 * mode_gain[16 * w : 16 * w + 16]
            cross = mm(gain, half)
            grams[w] = grams[w] + (cross + cross.T)
        mode_rows = mode_rows + mode_gain[0:16]
        moments = moments + mode_gain[112:120]
    return grams, mode_rows, moments


def shifted_stack(p, stack_ref, mine, lower, upper, yl_ref, yh_ref, zl_ref, zh_ref):
    lane = iota((RANK, 128), 1)
    field = mine[...]
    stack_ref[0:64, :] = field
    stack_ref[64:128, :] = lower[...]
    stack_ref[256:320, :] = upper[...]
    n = field.shape[1] // 128
    zl, zh = zl_ref[...], zh_ref[...]
    for y in range(n):
        here = field[:, 128 * y : 128 * y + 128]
        cols = slice(128 * y, 128 * y + 128)
        halo = slice(128 * p, 128 * p + 128)
        stack_ref[128:192, cols] = yl_ref[:, halo] if y == 0 else field[:, 128 * (y - 1) : 128 * y]
        stack_ref[320:384, cols] = (
            yh_ref[:, halo] if y == n - 1 else field[:, 128 * (y + 1) : 128 * (y + 2)]
        )
        g = p * n + y
        low = pltpu.roll(zl, (128 - g) % 128, 1)
        stack_ref[192:256, cols] = jnp.where(lane == 0, low, pltpu.roll(here, 1, 1))
        high = pltpu.roll(zh, 127 - g, 1)
        stack_ref[384:448, cols] = jnp.where(lane == 127, high, pltpu.roll(here, 127, 1))


def maps_kernel(
    first, count, cells, sums_ref, base_ref, cons_ref, fa, fb, xh, yl, yh, zl, zh,
    kb_ref, map_ref, sel_ref, seln_ref, gw_ref, mode_ref, mom_ref, civ_ref, ginv_ref, gain_ref,
    stack_ref,
):
    sums, base, cons = sums_ref[...], base_ref[...], cons_ref[...]
    gain = None
    if not first:
        gain = (TIME_STEP / cells) * mmt(base, sums[136:152, 64:128])
        gain_ref[...] = gain
    else:
        gain_ref[...] = jnp.zeros_like(gain_ref)
    grams, mode_rows, moments = symmetric(sums, gain, cons)
    shifted_stack(1, stack_ref, fb, fa, xh, yl, yh, zl, zh)
    times = mmt if first else mm
    sides = times(jnp.concatenate(grams, axis=0), base)
    sides = [sides[64 * w : 64 * w + 64] for w in range(7)]
    stay = (1.0 - TIME_STEP) * sides[0]
    for d in range(3):
        stay = stay + TIME_STEP * (sides[2 * d + 2] - sides[2 * d + 1])
    row = [stay] + [TIME_STEP * sides[2 * d + 1] for d in range(3)]
    row += [-TIME_STEP * sides[2 * d + 2] for d in range(3)] + [TIME_STEP * mode_rows.T]
    row = jnp.concatenate(row, axis=1) * (1.0 / count)
    sel = mm(cons[120:152, 0:8], times(moments, base) * (1.0 / count))
    sel_ref[...] = sel
    stack_ref[448:464, :] = features(sel, fb[...])
    gw_ref[...] = jnp.concatenate(grams[1:], axis=1)
    mode_ref[...] = mode_rows
    mom_ref[...] = moments
    _, civ = chol_inverse(grams[0] * (1.0 / count))
    maps = mm(civ, row)
    kb_ref[...] = mm(maps, stack_ref[...])
    map_ref[...] = maps
    civ_ref[...] = civ
    ginv_ref[...] = mm(civ.T, civ) * (1.0 / count)
    seln_ref[...] = mm(cons[120:152, 0:8], mmt(moments, civ) * (1.0 / count))


def columns(fields, lane_at):
    lane = iota((RANK, 128), 1)
    out = jnp.zeros((RANK, 128), F32)
    g = 0
    for field in fields:
        for y in range(field.shape[1] // 128):
            here = field[:, 128 * y : 128 * y + 128]
            out = jnp.where(lane == g, pltpu.roll(here, (g - lane_at) % 128, 1), out)
            g += 1
    return out


def plane_kernel(
    map_ref, sel_ref, fa, fb, xl, yl, yh, zl, zh, kb,
    ka_ref, ylo_ref, yho_ref, zlo_ref, zho_ref, stack_ref,
):
    shifted_stack(0, stack_ref, fa, xl, fb, yl, yh, zl, zh)
    stack_ref[448:464, :] = features(sel_ref[...], fa[...])
    ka = mm(map_ref[...], stack_ref[...])
    ka_ref[...] = ka
    kb = kb[...]
    n = ka.shape[1]
    ylo_ref[...] = jnp.concatenate([ka[:, n - 128 :], kb[:, n - 128 :]], axis=1)
    yho_ref[...] = jnp.concatenate([ka[:, :128], kb[:, :128]], axis=1)
    zlo_ref[...] = columns((ka, kb), 127)
    zho_ref[...] = columns((ka, kb), 0)


def inner_kernel(seln_ref, ka, kb, out_ref, stack_ref):
    lane = iota((RANK, 128), 1)
    n = ka.shape[1]
    zero = jnp.zeros((RANK, 128), F32)
    for p, ref in enumerate((ka, kb)):
        at = p * n
        field = ref[...]
        stack_ref[0:64, at : at + n] = field
        stack_ref[128:192, at : at + 128] = zero
        stack_ref[128:192, at + 128 : at + n] = field[:, : n - 128]
        for y in range(n // 128):
            here = field[:, 128 * y : 128 * y + 128]
            stack_ref[192:256, at + 128 * y : at + 128 * y + 128] = jnp.where(
                lane == 0, 0.0, pltpu.roll(here, 1, 1)
            )
        stack_ref[256:272, at : at + n] = features(seln_ref[...], field)
    stack_ref[64:128, 0:n] = jnp.zeros((RANK, n), F32)
    stack_ref[64:128, n : 2 * n] = ka[...]
    out_ref[...] = mmt(stack_ref[...], stack_ref[0:64, :])


def edge_kernel(part_ref, ka, xl, yl, yh, zl, zh, out_ref):
    part = part_ref[...]
    out_ref[...] = jnp.zeros_like(out_ref)
    out_ref[0:64, 0:64] = part[0:64]
    out_ref[0:64, 64:128] = part[64:128] + mmt(xl[...], ka[...])
    out_ref[64:128, 0:64] = part[128:192] + mmt(yl[...], yh[...])
    out_ref[64:128, 64:128] = part[192:256] + mmt(zl[...], zh[...])
    out_ref[128:144, 0:64] = part[256:272]


def core_kernel(
    first, last, count, cells, nz, v1_ref, sums_ref, ka, kb, rows_ref, gain_ref, tab_ref, cons_ref,
    gw_ref, mode_ref, mom_ref, civ_ref, ginv_ref, out_ref, rows_out, cxi_ref, stack_ref, base_ref,
):
    v1 = v1_ref[0, 0]
    rows = rows_ref[...]
    if not first:
        rows = rows + mm(gain_ref[...], tab_ref[0:16, :])
    v2, v3 = tab_ref[18:19, :], tab_ref[19:20, :]
    base_ref[0:64, :] = rows
    base_ref[64:128, :] = rows * jnp.maximum(v2, 0.0)
    base_ref[128:192, :] = rows * jnp.minimum(v2, 0.0)
    base_ref[192:256, :] = rows * jnp.maximum(v3, 0.0)
    base_ref[256:320, :] = rows * jnp.minimum(v3, 0.0)
    sums = sums_ref[...] * (1.0 / cells)
    civ = civ_ref[...]
    unit = eye()
    up, cxi = chol_inverse(sums[0:64, 0:64])
    cxi_ref[...] = cxi
    y = mm(up, civ)
    zs = jnp.concatenate([sums[0:64, 64:128], sums[64:128, 0:64], sums[64:128, 64:128]], axis=0)
    zs = mmt(zs, cxi)
    lower, upper = [], []
    for d in range(3):
        turned = mm(cxi, zs[64 * d : 64 * d + 64])
        lower.append(unit - turned.T)
        upper.append(turned - unit)
    yg = mm(y, gw_ref[...])
    yg = jnp.concatenate([yg[:, 64 * w : 64 * w + 64] for w in range(6)], axis=0)
    sides = jnp.concatenate([lower[0], upper[0], lower[1], upper[1], lower[2], upper[2]], axis=1)
    rate = mm(mmt(cxi, sums[128:144, 0:64]), mode_ref[...]) - mm(sides, yg)
    y = (1.0 + TIME_STEP) * y - TIME_STEP * mm(rate, ginv_ref[...])
    sel = mm(cons_ref[120:152, 0:8], mm(mmt(mom_ref[...], y) * (1.0 / count), cxi))
    collide = mmt(features(sel, ka[...]), ka[...]) + mmt(features(sel, kb[...]), kb[...])
    turn = lower[0] * jnp.maximum(v1, 0.0) + upper[0] * jnp.minimum(v1, 0.0)
    move = [(1.0 - TIME_STEP) * unit - TIME_STEP * turn]
    move += [-TIME_STEP * m for m in (lower[1], upper[1], lower[2], upper[2])]
    move = mm(jnp.concatenate(move, axis=0), y)
    move = jnp.concatenate([move[64 * t : 64 * t + 64] for t in range(5)], axis=1)
    rows = mm(move, base_ref[...])
    rows_out[...] = rows
    weighted_payload(rows, v1, tab_ref, out_ref, stack_ref, 1.0 / nz, collide, not last)


def finish_kernel(count, cells, sums_ref, cxi_ref, rows_ref, tab_ref, cons_ref, low_ref, out_ref):
    sums = sums_ref[...]
    gain = (TIME_STEP / cells) * mmt(cxi_ref[...], sums[136:152, 64:128])
    half = sums[128:144, 0:64] + 0.5 * mmt(cons_ref[0:16, :], gain)
    cross = mm(gain, half)
    up, civ = chol_inverse((sums[0:64, 0:64] + (cross + cross.T)) * (1.0 / count))
    low_ref[...] = up.T
    out_ref[...] = mm(civ, rows_ref[...] + mm(gain, tab_ref[0:16, :]))


def call(kernel, outs, scratch, *args):
    shapes = [jax.ShapeDtypeStruct(s, F32) for s in outs]
    specs = [pl.BlockSpec(memory_space=pltpu.VMEM) for _ in args]
    if args[0].shape == (1, 1):
        specs[0] = pl.BlockSpec(memory_space=pltpu.SMEM)
    return pl.pallas_call(
        kernel,
        out_shape=shapes,
        in_specs=specs,
        out_specs=[pl.BlockSpec(memory_space=pltpu.VMEM) for _ in outs],
        scratch_shapes=[pltpu.VMEM(s, F32) for s in scratch],
        compiler_params=pltpu.CompilerParams(vmem_limit_bytes=40 * 1024 * 1024),
    )(*args)


def route(axis, step):
    n = lax.axis_size(axis)
    return [(i, (i + step) % n) for i in range(n)]


def swap(chunks, axis):
    return lax.all_to_all(chunks, axis, 0, 0, tiled=True)


def total(payload, over_z):
    n = lax.axis_size(PLANE)
    rows = payload.shape[0] // n
    part = jnp.sum(swap(payload.reshape(n, rows, 128), PLANE), axis=0)
    if over_z:
        nz = lax.axis_size("bz")
        part = jnp.sum(swap(jnp.broadcast_to(part[None], (nz, rows, 128)), "bz"), axis=0)
    return swap(jnp.broadcast_to(part[None], (n, rows, 128)), PLANE).reshape(n * rows, 128)


def local(space_factor, core_matrix, velocity_factor):
    vel_rows = velocity_factor.shape[1]
    plane = lax.axis_index(PLANE)
    count = vel_rows * lax.axis_size(PLANE)
    nz = lax.axis_size("bz")
    shape = space_factor.shape
    half = shape[2] * shape[3]
    cells = 2 * half * lax.axis_size(PLANE) * nz
    cons = jnp.asarray(constants(count))
    digit = (plane * vel_rows) // (VEL_N * VEL_N)
    v1 = SPEED_MAX * (2.0 * digit.astype(F32) + 1.0 - VEL_N) / VEL_N
    v1 = v1.reshape(1, 1)

    fa = space_factor[:, 0].reshape(RANK, half)
    fb = space_factor[:, 1].reshape(RANK, half)
    payload, tab = call(
        start_kernel, [(256, 128), (24, vel_rows)], [(408, vel_rows)], v1, velocity_factor
    )
    yl = space_factor[:, :, -1].reshape(RANK, 256)
    yh = space_factor[:, :, 0].reshape(RANK, 256)
    pad = jnp.zeros((RANK, 128 - 2 * shape[2]), F32)
    zl = jnp.concatenate([space_factor[:, :, :, -1].reshape(RANK, -1), pad], axis=1)
    zh = jnp.concatenate([space_factor[:, :, :, 0].reshape(RANK, -1), pad], axis=1)

    def low_halo(xl, yl, zl):
        return (
            lax.ppermute(xl, "bx", route("bx", 1)),
            lax.ppermute(yl, "by", route("by", 1)),
            lax.ppermute(zl, "bz", route("bz", 1)),
        )

    def high_halo(xh, yh, zh):
        return (
            lax.ppermute(xh, "bx", route("bx", -1)),
            lax.ppermute(yh, "by", route("by", -1)),
            lax.ppermute(zh, "bz", route("bz", -1)),
        )

    low = low_halo(fb, yl, zl)
    high = high_halo(fa, yh, zh)
    sums = total(payload, False)
    base, rows = core_matrix, velocity_factor
    for turn in range(STEPS):
        first, last = turn == 0, turn + 1 == STEPS
        kb, maps, sel, seln, gw, mode_rows, moments, civ, ginv, gain = call(
            functools.partial(maps_kernel, first, count, cells),
            [(RANK, half), (RANK, 464), (32, RANK), (32, RANK), (RANK, 384), (16, RANK), (8, RANK),
             (RANK, RANK), (RANK, RANK), (RANK, 16)],
            [(464, half)],
            sums, base, cons, fa, fb, high[0], low[1], high[1], low[2], high[2],
        )
        ka, yl, yh, zl, zh = call(
            plane_kernel,
            [(RANK, half), (RANK, 256), (RANK, 256), (RANK, 128), (RANK, 128)],
            [(464, half)],
            maps, sel, fa, fb, low[0], low[1], high[1], low[2], high[2], kb,
        )
        low = low_halo(kb, yl, zl)
        (part,) = call(inner_kernel, [(272, RANK)], [(272, 2 * half)], seln, ka, kb)
        (payload,) = call(edge_kernel, [(256, 128)], [], part, ka, low[0], low[1], yh, low[2], zh)
        fa, fb = ka, kb
        if not last:
            high = high_halo(ka, yh, zh)
        sums = total(payload, True)
        payload, rows, base = call(
            functools.partial(core_kernel, first, last, count, cells, nz),
            [(256, 128), (RANK, vel_rows), (RANK, RANK)],
            [(408, vel_rows), (320, vel_rows)],
            v1, sums, ka, kb, rows, gain, tab, cons, gw, mode_rows, moments, civ, ginv,
        )
        sums = total(payload, True)
    new_space = jnp.stack(
        [mm(base, ka).reshape(RANK, *shape[2:]), mm(base, kb).reshape(RANK, *shape[2:])], axis=1
    )
    new_core, new_velocity = call(
        functools.partial(finish_kernel, count, cells),
        [(RANK, RANK), (RANK, vel_rows)], [], sums, base, rows, tab, cons,
    )
    return new_space, new_core, new_velocity


def solution(mesh):
    return jax.shard_map(
        local,
        mesh=mesh,
        in_specs=(P(None, "bx", "by", "bz"), P(), P(None, PLANE)),
        out_specs=(P(None, "bx", "by", "bz"), P(), P(None, PLANE)),
        check_vma=False,
    )
```

```python
import functools

import jax
import jax.numpy as jnp
import numpy as np
from jax import lax
from jax.experimental import pallas as pl
from jax.experimental.pallas import tpu as pltpu
from jax.sharding import PartitionSpec as P

VEL_N = 32
STEPS = 2
TIME_STEP = 0.1
SPEED_MAX = 3.0
HIGHEST = lax.Precision.HIGHEST
PLANE = ("bx", "by")
RANK = 64
F32 = jnp.float32


def mm(a, b):
    return jnp.dot(a, b, precision=HIGHEST, preferred_element_type=F32)


def mmt(a, b):
    return lax.dot_general(
        a, b, (((1,), (1,)), ((), ())), precision=HIGHEST, preferred_element_type=F32
    )


def np_tables(row_total):
    row_ids = np.arange(row_total)
    levels = np.stack([row_ids // (VEL_N * VEL_N), row_ids // VEL_N % VEL_N, row_ids % VEL_N])
    v = SPEED_MAX * (2.0 * levels + 1.0 - VEL_N) / VEL_N
    w = np.exp(-0.5 * np.sum(v * v, axis=0)) / line_mean() ** 3
    modes = np.stack(
        [w, w * v[0], w * v[1], w * v[2]]
        + [0.5 * w * (v[d] * v[d] - 1.0) for d in range(3)]
        + [w * v[0] * v[1], w * v[0] * v[2], w * v[1] * v[2]]
    )
    weights = [np.ones_like(w)]
    for d in range(3):
        weights += [np.maximum(v[d], 0.0), np.minimum(v[d], 0.0)]
    return v, modes, np.stack(weights)


def line_mean():
    line = SPEED_MAX * (2.0 * np.arange(VEL_N) + 1.0 - VEL_N) / VEL_N
    return float(np.mean(np.exp(-0.5 * line * line)))


def constants(row_total):
    v, modes, weights = np_tables(row_total)
    gram = np.einsum("wv,mv,nv->wmn", weights, modes, modes)
    out = np.zeros((160, 16), np.float32)
    for w in range(7):
        out[16 * w : 16 * w + 10, :10] = gram[w]
    out[112, :10] = modes.sum(axis=1)
    for d in range(3):
        out[113 + d, :10] = modes @ v[d]
    first = [0, 1, 2, 3, 1, 2, 3, 1, 1, 2]
    second = [None, None, None, None, 1, 2, 3, 2, 3, 3]
    for r in range(10):
        out[120 + r, first[r]] = 1.0
        if second[r] is not None:
            out[136 + r, second[r]] = 1.0
    return out


def iota(shape, dim):
    return lax.broadcasted_iota(jnp.int32, shape, dim)


def eye():
    return (iota((RANK, RANK), 0) == iota((RANK, RANK), 1)).astype(F32)


def spread_lane(block, k):
    return jnp.broadcast_to(block[:, k : k + 1], (8, 128))


def spread_row(block, r):
    return jnp.broadcast_to(block[r : r + 1, :], (8, 128))


def chol_inverse(gram, width=4):
    lane = iota((8, 128), 1)
    sub = iota((8, 128), 0)
    on_diag = gram * eye()
    diag = jnp.sum(on_diag, axis=0, keepdims=True)
    row_scale = lax.rsqrt(diag)
    scaled = gram * row_scale * lax.rsqrt(jnp.sum(on_diag, axis=1, keepdims=True))
    wide = jnp.concatenate([scaled, jnp.zeros_like(gram)], axis=1)
    blocks = []
    for b in range(8):
        unit = jnp.where(lane == sub + (64 + 8 * b), 1.0, 0.0)
        blocks.append(wide[8 * b : 8 * b + 8] + unit)
    for k in range(0, RANK, width):
        b, r = divmod(k, 8)
        left = range(b, 8)
        cols = [{i: spread_lane(blocks[i], k + j) for i in left} for j in range(width)]
        heads = [spread_row(blocks[b], r + j) for j in range(width)]
        for j in range(0, width, 2):
            p = spread_row(cols[j][b], r + j)
            q = spread_row(cols[j][b], r + j + 1)
            s = spread_row(cols[j + 1][b], r + j + 1)
            inv_p = lax.rsqrt(p)
            both = inv_p * lax.rsqrt(p * s - q * q)
            pb, qb = both * p, both * q
            for i in left:
                first = cols[j][i]
                cols[j][i] = first * inv_p
                cols[j + 1][i] = pb * cols[j + 1][i] - qb * first
            first = heads[j]
            heads[j] = first * inv_p
            heads[j + 1] = pb * heads[j + 1] - qb * first
            for m in range(j + 2, width):
                u = spread_row(cols[j][b], r + m)
                w = spread_row(cols[j + 1][b], r + m)
                for i in left:
                    cols[m][i] = (cols[m][i] - cols[j][i] * u) - cols[j + 1][i] * w
                heads[m] = (heads[m] - heads[j] * u) - heads[j + 1] * w
        for i in left:
            if i == b and r + width == 8:
                new = blocks[i]
            else:
                new = blocks[i]
                for j in range(width):
                    new = new - cols[j][i] * heads[j]
            if i == b:
                new = jnp.where(sub >= r + width, new, blocks[i])
                for j in range(width):
                    new = jnp.where(sub == r + j, heads[j], new)
            blocks[i] = new
    full = jnp.concatenate(blocks, axis=0)
    keep = iota((RANK, RANK), 1) >= iota((RANK, RANK), 0)
    upper = jnp.where(keep, full[:, :RANK], 0.0) * (diag * row_scale)
    return upper, full[:, RANK:] * row_scale


def features(sel_map, field):
    both = mm(sel_map, field)
    lift = jnp.where(iota((16, field.shape[1]), 0) < 4, 1.0, 0.0)
    return both[:16] * (both[16:] + lift)


def pair_block(plus, minus):
    return jnp.where(iota((RANK, RANK), 0) <= iota((RANK, RANK), 1), plus, minus)


def tables_kernel(v1_ref, tab_ref):
    lanes = tab_ref.shape[1]
    at = iota((1, lanes), 1)
    v2 = SPEED_MAX * (2.0 * (at // VEL_N).astype(F32) + 1.0 - VEL_N) / VEL_N
    v3 = SPEED_MAX * (2.0 * (at % VEL_N).astype(F32) + 1.0 - VEL_N) / VEL_N
    v1 = jnp.full((1, lanes), v1_ref[0, 0], F32)
    w = jnp.exp(-0.5 * (v1 * v1 + v2 * v2 + v3 * v3)) / (line_mean() ** 3)
    tab_ref[...] = jnp.zeros_like(tab_ref)
    modes = [w, w * v1, w * v2, w * v3]
    modes += [0.5 * w * (v * v - 1.0) for v in (v1, v2, v3)]
    modes += [w * v1 * v2, w * v1 * v3, w * v2 * v3]
    for i, m in enumerate(modes):
        tab_ref[i : i + 1, :] = m
    for i, m in enumerate([jnp.ones_like(v1), v1, v2, v3]):
        tab_ref[16 + i : 17 + i, :] = m


def weigh_kernel(scale, v1_ref, rows_ref, tab_ref, coll_ref, out_ref, stack_ref, res_ref):
    v1 = v1_ref[0, 0]
    lanes = rows_ref.shape[1]
    width = lanes // 4
    res_ref[...] = jnp.zeros_like(res_ref)

    def chunk(c, carry):
        cols = pl.ds(pl.multiple_of(c * width, width), width)
        rows, modes = rows_ref[:, cols], tab_ref[0:16, cols]
        v2, v3 = tab_ref[18:19, cols], tab_ref[19:20, cols]
        weights = [None, jnp.maximum(v2, 0.0), jnp.minimum(v2, 0.0)]
        weights += [jnp.maximum(v3, 0.0), jnp.minimum(v3, 0.0)]
        for i, w in enumerate(weights):
            stack_ref[80 * i : 80 * i + 64, :] = rows if w is None else rows * w
            stack_ref[80 * i + 64 : 80 * i + 80, :] = modes if w is None else modes * w
        stack_ref[400:408, :] = tab_ref[16:24, cols]
        res_ref[...] += mmt(stack_ref[...], rows)
        return carry

    lax.fori_loop(0, 4, chunk, 0)
    quads = [res_ref[80 * i : 80 * i + 64, :] * scale for i in range(5)]
    cross = [res_ref[80 * i + 64 : 80 * i + 80, :] * scale for i in range(5)]
    out_ref[...] = jnp.zeros_like(out_ref)
    out_ref[0:64, 0:64] = quads[0]
    out_ref[128:144, 0:64] = cross[0]
    v1p, v1m = jnp.maximum(v1, 0.0), jnp.minimum(v1, 0.0)
    pairs = [(quads[0] * v1p, quads[0] * v1m), (quads[1], quads[2]), (quads[3], quads[4])]
    crosses = [cross[0] * v1p, cross[0] * v1m] + cross[1:]
    out_ref[0:64, 64:128] = pair_block(*pairs[1])
    out_ref[64:128, 0:64] = pair_block(*pairs[0])
    out_ref[64:128, 64:128] = pair_block(*pairs[2])
    for i in range(6):
        out_ref[144 + 16 * i : 160 + 16 * i, 0:64] = crosses[i]
    out_ref[128:136, 64:128] = res_ref[400:408, :] * scale
    out_ref[136:152, 64:128] = coll_ref[...]
    for d in range(3):
        out_ref[152 + d : 153 + d, 64:128] = jnp.sum(pairs[d][1] * eye(), axis=0, keepdims=True)


def symmetric(sums, gain, cons):
    upper = iota((RANK, RANK), 0) <= iota((RANK, RANK), 1)
    diag = iota((RANK, RANK), 0) == iota((RANK, RANK), 1)
    packs = [sums[64:128, 0:64], sums[0:64, 64:128], sums[64:128, 64:128]]
    grams = [sums[0:64, 0:64]]
    for d in range(3):
        turned = packs[d].T
        grams.append(jnp.where(upper, packs[d], turned))
        grams.append(
            jnp.where(diag, sums[152 + d : 153 + d, 64:128], jnp.where(upper, turned, packs[d]))
        )
    mode_gain = mmt(cons[0:120], gain)
    for w in range(7):
        half = sums[128 + 16 * w : 144 + 16 * w, 0:64] + 0.5 * mode_gain[16 * w : 16 * w + 16]
        cross = mm(gain, half)
        grams[w] = grams[w] + (cross + cross.T)
    mode_rows = sums[128:144, 0:64] + mode_gain[0:16]
    moments = sums[128:136, 64:128] + mode_gain[112:120]
    return grams, mode_rows, moments


def shifted_stack(p, stack_ref, mine, lower, upper, yl_ref, yh_ref, zl_ref, zh_ref):
    lane = iota((RANK, 128), 1)
    field = mine[...]
    stack_ref[0:64, :] = field
    stack_ref[64:128, :] = lower[...]
    stack_ref[256:320, :] = upper[...]
    n = field.shape[1] // 128
    zl, zh = zl_ref[...], zh_ref[...]
    for y in range(n):
        here = field[:, 128 * y : 128 * y + 128]
        cols = slice(128 * y, 128 * y + 128)
        halo = slice(128 * p, 128 * p + 128)
        stack_ref[128:192, cols] = yl_ref[:, halo] if y == 0 else field[:, 128 * (y - 1) : 128 * y]
        stack_ref[320:384, cols] = (
            yh_ref[:, halo] if y == n - 1 else field[:, 128 * (y + 1) : 128 * (y + 2)]
        )
        g = p * n + y
        low = pltpu.roll(zl, (128 - g) % 128, 1)
        stack_ref[192:256, cols] = jnp.where(lane == 0, low, pltpu.roll(here, 1, 1))
        high = pltpu.roll(zh, 127 - g, 1)
        stack_ref[384:448, cols] = jnp.where(lane == 127, high, pltpu.roll(here, 127, 1))


def maps_kernel(
    count, cells, sums_ref, base_ref, cons_ref, fa, fb, xh, yl, yh, zl, zh,
    kb_ref, map_ref, sel_ref, seln_ref, gw_ref, mode_ref, mom_ref, civ_ref, ginv_ref, gain_ref,
    stack_ref,
):
    sums, base, cons = sums_ref[...], base_ref[...], cons_ref[...]
    gain = (TIME_STEP / cells) * mmt(base, sums[136:152, 64:128])
    gain_ref[...] = gain
    grams, mode_rows, moments = symmetric(sums, gain, cons)
    shifted_stack(1, stack_ref, fb, fa, xh, yl, yh, zl, zh)
    sides = mm(jnp.concatenate(grams, axis=0), base)
    sides = [sides[64 * w : 64 * w + 64] for w in range(7)]
    stay = (1.0 - TIME_STEP) * sides[0]
    for d in range(3):
        stay = stay + TIME_STEP * (sides[2 * d + 2] - sides[2 * d + 1])
    row = [stay] + [TIME_STEP * sides[2 * d + 1] for d in range(3)]
    row += [-TIME_STEP * sides[2 * d + 2] for d in range(3)] + [TIME_STEP * mode_rows.T]
    row = jnp.concatenate(row, axis=1) * (1.0 / count)
    sel = mm(cons[120:152, 0:8], mm(moments, base) * (1.0 / count))
    sel_ref[...] = sel
    stack_ref[448:464, :] = features(sel, fb[...])
    gw_ref[...] = jnp.concatenate(grams[1:], axis=1)
    mode_ref[...] = mode_rows
    mom_ref[...] = moments
    _, civ = chol_inverse(grams[0] * (1.0 / count))
    maps = mm(civ, row)
    kb_ref[...] = mm(maps, stack_ref[...])
    map_ref[...] = maps
    civ_ref[...] = civ
    ginv_ref[...] = mm(civ.T, civ) * (1.0 / count)
    seln_ref[...] = mm(cons[120:152, 0:8], mmt(moments, civ) * (1.0 / count))


def columns(fields, lane_at):
    lane = iota((RANK, 128), 1)
    out = jnp.zeros((RANK, 128), F32)
    g = 0
    for field in fields:
        for y in range(field.shape[1] // 128):
            here = field[:, 128 * y : 128 * y + 128]
            out = jnp.where(lane == g, pltpu.roll(here, (g - lane_at) % 128, 1), out)
            g += 1
    return out


def plane_kernel(
    map_ref, sel_ref, fa, fb, xl, yl, yh, zl, zh, kb,
    ka_ref, ylo_ref, yho_ref, zlo_ref, zho_ref, stack_ref,
):
    shifted_stack(0, stack_ref, fa, xl, fb, yl, yh, zl, zh)
    stack_ref[448:464, :] = features(sel_ref[...], fa[...])
    ka = mm(map_ref[...], stack_ref[...])
    ka_ref[...] = ka
    kb = kb[...]
    n = ka.shape[1]
    ylo_ref[...] = jnp.concatenate([ka[:, n - 128 :], kb[:, n - 128 :]], axis=1)
    yho_ref[...] = jnp.concatenate([ka[:, :128], kb[:, :128]], axis=1)
    zlo_ref[...] = columns((ka, kb), 127)
    zho_ref[...] = columns((ka, kb), 0)


def inner_kernel(seln_ref, ka, kb, out_ref, stack_ref):
    lane = iota((RANK, 128), 1)
    n = ka.shape[1]
    zero = jnp.zeros((RANK, 128), F32)
    for p, ref in enumerate((ka, kb)):
        at = p * n
        field = ref[...]
        stack_ref[0:64, at : at + n] = field
        stack_ref[128:192, at : at + 128] = zero
        stack_ref[128:192, at + 128 : at + n] = field[:, : n - 128]
        for y in range(n // 128):
            here = field[:, 128 * y : 128 * y + 128]
            stack_ref[192:256, at + 128 * y : at + 128 * y + 128] = jnp.where(
                lane == 0, 0.0, pltpu.roll(here, 1, 1)
            )
        stack_ref[256:272, at : at + n] = features(seln_ref[...], field)
    stack_ref[64:128, 0:n] = jnp.zeros((RANK, n), F32)
    stack_ref[64:128, n : 2 * n] = ka[...]
    out_ref[...] = jnp.zeros_like(out_ref)
    width = n // 2

    def chunk(c, carry):
        cols = pl.ds(pl.multiple_of(c * width, width), width)
        out_ref[...] += mmt(stack_ref[:, cols], stack_ref[0:64, cols])
        return carry

    lax.fori_loop(0, 4, chunk, 0)


def edge_kernel(part_ref, ka, xl, yl, yh, zl, zh, out_ref):
    part = part_ref[...]
    out_ref[0:64, 0:64] = part[0:64]
    out_ref[32:48, 0:32] = part[256:272, 0:32]
    out_ref[48:64, 0:32] = part[256:272, 32:64]
    out_ref[0:64, 64:128] = part[64:128] + mmt(xl[...], ka[...])
    out_ref[64:128, 0:64] = part[128:192] + mmt(yl[...], yh[...])
    out_ref[64:128, 64:128] = part[192:256] + mmt(zl[...], zh[...])


def core_kernel(
    count, cells, v1_ref, sums_ref, ka, kb, rows_ref, gain_ref, tab_ref, cons_ref,
    gw_ref, mode_ref, mom_ref, civ_ref, ginv_ref, coll_ref, rows_out, cxi_ref, base_ref,
):
    v1 = v1_ref[0, 0]
    rows = rows_ref[...] + mm(gain_ref[...], tab_ref[0:16, :])
    v2, v3 = tab_ref[18:19, :], tab_ref[19:20, :]
    base_ref[0:64, :] = rows
    base_ref[64:128, :] = rows * jnp.maximum(v2, 0.0)
    base_ref[128:192, :] = rows * jnp.minimum(v2, 0.0)
    base_ref[192:256, :] = rows * jnp.maximum(v3, 0.0)
    base_ref[256:320, :] = rows * jnp.minimum(v3, 0.0)
    sums = sums_ref[...] * (1.0 / cells)
    civ = civ_ref[...]
    unit = eye()
    gram = sums[0:64, 0:64]
    corner = (iota((RANK, RANK), 0) >= 32) & (iota((RANK, RANK), 1) < 32)
    up, cxi = chol_inverse(jnp.where(corner, gram.T, gram))
    cxi_ref[...] = cxi
    moment_x = jnp.concatenate([sums[32:48, 0:32], sums[48:64, 0:32]], axis=1)
    y = mm(up, civ)
    zs = jnp.concatenate([sums[0:64, 64:128], sums[64:128, 0:64], sums[64:128, 64:128]], axis=0)
    zs = mmt(zs, cxi)
    lower, upper = [], []
    for d in range(3):
        turned = mm(cxi, zs[64 * d : 64 * d + 64])
        lower.append(unit - turned.T)
        upper.append(turned - unit)
    yg = mm(y, gw_ref[...])
    yg = jnp.concatenate([yg[:, 64 * w : 64 * w + 64] for w in range(6)], axis=0)
    sides = jnp.concatenate([lower[0], upper[0], lower[1], upper[1], lower[2], upper[2]], axis=1)
    rate = mm(mmt(cxi, moment_x), mode_ref[...]) - mm(sides, yg)
    y = (1.0 + TIME_STEP) * y - TIME_STEP * mm(rate, ginv_ref[...])
    sel = mm(cons_ref[120:152, 0:8], mm(mmt(mom_ref[...], y) * (1.0 / count), cxi))
    collide = mmt(features(sel, ka[...]), ka[...]) + mmt(features(sel, kb[...]), kb[...])
    turn = lower[0] * jnp.maximum(v1, 0.0) + upper[0] * jnp.minimum(v1, 0.0)
    move = [(1.0 - TIME_STEP) * unit - TIME_STEP * turn]
    move += [-TIME_STEP * m for m in (lower[1], upper[1], lower[2], upper[2])]
    move = mm(jnp.concatenate(move, axis=0), y)
    move = jnp.concatenate([move[64 * t : 64 * t + 64] for t in range(5)], axis=1)
    rows_out[...] = mm(move, base_ref[...])
    coll_ref[...] = collide


def finish_kernel(count, cells, sums_ref, cxi_ref, rows_ref, tab_ref, cons_ref, low_ref, out_ref):
    sums = sums_ref[...]
    gain = (TIME_STEP / cells) * mmt(cxi_ref[...], sums[136:152, 64:128])
    half = sums[128:144, 0:64] + 0.5 * mmt(cons_ref[0:16, :], gain)
    cross = mm(gain, half)
    up, civ = chol_inverse((sums[0:64, 0:64] + (cross + cross.T)) * (1.0 / count))
    low_ref[...] = up.T
    out_ref[...] = mm(civ, rows_ref[...] + mm(gain, tab_ref[0:16, :]))


def call(kernel, outs, scratch, *args):
    shapes = [jax.ShapeDtypeStruct(s, F32) for s in outs]
    specs = [pl.BlockSpec(memory_space=pltpu.VMEM) for _ in args]
    if args[0].shape == (1, 1):
        specs[0] = pl.BlockSpec(memory_space=pltpu.SMEM)
    return pl.pallas_call(
        kernel,
        out_shape=shapes,
        in_specs=specs,
        out_specs=[pl.BlockSpec(memory_space=pltpu.VMEM) for _ in outs],
        scratch_shapes=[pltpu.VMEM(s, F32) for s in scratch],
        compiler_params=pltpu.CompilerParams(vmem_limit_bytes=40 * 1024 * 1024),
    )(*args)


def route(axis, step):
    n = lax.axis_size(axis)
    return [(i, (i + step) % n) for i in range(n)]


def swap(chunks, axis):
    return lax.all_to_all(chunks, axis, 0, 0, tiled=True)


def spread(part, n):
    return jnp.broadcast_to(part[None], (n,) + part.shape)


def plane_sum(payload):
    n = lax.axis_size(PLANE)
    return jnp.sum(swap(payload.reshape(n, -1, 128), PLANE), axis=0)


def line_sum(part):
    return jnp.sum(swap(spread(part, lax.axis_size("bz")), "bz"), axis=0)


def plane_gather(part):
    return swap(spread(part, lax.axis_size(PLANE)), PLANE).reshape(-1, 128)


def local(space_factor, core_matrix, velocity_factor):
    vel_rows = velocity_factor.shape[1]
    plane = lax.axis_index(PLANE)
    count = vel_rows * lax.axis_size(PLANE)
    nz = lax.axis_size("bz")
    shape = space_factor.shape
    half = shape[2] * shape[3]
    cells = 2 * half * lax.axis_size(PLANE) * nz
    cons = jnp.asarray(constants(count))
    digit = (plane * vel_rows) // (VEL_N * VEL_N)
    v1 = SPEED_MAX * (2.0 * digit.astype(F32) + 1.0 - VEL_N) / VEL_N
    v1 = v1.reshape(1, 1)

    fa = space_factor[:, 0].reshape(RANK, half)
    fb = space_factor[:, 1].reshape(RANK, half)
    (tab,) = call(tables_kernel, [(24, vel_rows)], [], v1)

    def weigh(rows, coll, scale):
        return call(
            functools.partial(weigh_kernel, scale),
            [(256, 128)], [(408, vel_rows // 4), (408, RANK)], v1, rows, tab, coll,
        )[0]

    payload = weigh(velocity_factor, jnp.zeros((16, RANK), F32), 1.0)
    yl = space_factor[:, :, -1].reshape(RANK, 256)
    yh = space_factor[:, :, 0].reshape(RANK, 256)
    pad = jnp.zeros((RANK, 128 - 2 * shape[2]), F32)
    zl = jnp.concatenate([space_factor[:, :, :, -1].reshape(RANK, -1), pad], axis=1)
    zh = jnp.concatenate([space_factor[:, :, :, 0].reshape(RANK, -1), pad], axis=1)

    def low_halo(xl, yl, zl):
        return (
            lax.ppermute(xl, "bx", route("bx", 1)),
            lax.ppermute(yl, "by", route("by", 1)),
            lax.ppermute(zl, "bz", route("bz", 1)),
        )

    def high_halo(xh, yh, zh):
        return (
            lax.ppermute(xh, "bx", route("bx", -1)),
            lax.ppermute(yh, "by", route("by", -1)),
            lax.ppermute(zh, "bz", route("bz", -1)),
        )

    low = low_halo(fb, yl, zl)
    high = high_halo(fa, yh, zh)
    sums = plane_gather(plane_sum(payload))

    def step(turn, carry):
        fa, fb, low, high, sums, rows, base = carry
        kb, maps, sel, seln, gw, mode_rows, moments, civ, ginv, gain = call(
            functools.partial(maps_kernel, count, cells),
            [(RANK, half), (RANK, 464), (32, RANK), (32, RANK), (RANK, 384), (16, RANK), (8, RANK),
             (RANK, RANK), (RANK, RANK), (RANK, 16)],
            [(464, half)],
            sums, base, cons, fa, fb, high[0], low[1], high[1], low[2], high[2],
        )
        ka, yl, yh, zl, zh = call(
            plane_kernel,
            [(RANK, half), (RANK, 256), (RANK, 256), (RANK, 128), (RANK, 128)],
            [(464, half)],
            maps, sel, fa, fb, low[0], low[1], high[1], low[2], high[2], kb,
        )
        low = low_halo(kb, yl, zl)
        (part,) = call(inner_kernel, [(272, RANK)], [(272, 2 * half)], seln, ka, kb)
        (payload,) = call(edge_kernel, [(128, 128)], [], part, ka, low[0], low[1], yh, low[2], zh)
        high = high_halo(ka, yh, zh)
        sums = plane_gather(line_sum(plane_sum(payload)))
        coll, rows, base = call(
            functools.partial(core_kernel, count, cells),
            [(16, RANK), (RANK, vel_rows), (RANK, RANK)],
            [(320, vel_rows)],
            v1, sums, ka, kb, rows, gain, tab, cons, gw, mode_rows, moments, civ, ginv,
        )
        sums = plane_gather(line_sum(plane_sum(weigh(rows, coll, 1.0 / nz))))
        return ka, kb, low, high, sums, rows, base

    carry = (fa, fb, low, high, sums, velocity_factor, core_matrix.T)
    ka, kb, _, _, sums, rows, base = lax.fori_loop(0, STEPS, step, carry)
    new_space = jnp.stack(
        [mm(base, ka).reshape(RANK, *shape[2:]), mm(base, kb).reshape(RANK, *shape[2:])], axis=1
    )
    new_core, new_velocity = call(
        functools.partial(finish_kernel, count, cells),
        [(RANK, RANK), (RANK, vel_rows)], [], sums, base, rows, tab, cons,
    )
    return new_space, new_core, new_velocity


def solution(mesh):
    return jax.shard_map(
        local,
        mesh=mesh,
        in_specs=(P(None, "bx", "by", "bz"), P(), P(None, PLANE)),
        out_specs=(P(None, "bx", "by", "bz"), P(), P(None, PLANE)),
        check_vma=False,
    )
```

```python
import functools

import jax
import jax.numpy as jnp
import numpy as np
from jax import lax
from jax.experimental import pallas as pl
from jax.experimental.pallas import tpu as pltpu
from jax.sharding import PartitionSpec as P


VEL_N = 32
STEPS = 2
TIME_STEP = 0.1
SPEED_MAX = 3.0
HIGHEST = lax.Precision.HIGHEST
PLANE = ("bx", "by")
RANK = 64
F32 = jnp.float32


def mm(a, b):
    return jnp.dot(a, b, precision=HIGHEST, preferred_element_type=F32)


def mmt(a, b):
    return lax.dot_general(
        a, b, (((1,), (1,)), ((), ())), precision=HIGHEST, preferred_element_type=F32
    )


def np_tables(row_total):
    row_ids = np.arange(row_total)
    levels = np.stack([row_ids // (VEL_N * VEL_N), row_ids // VEL_N % VEL_N, row_ids % VEL_N])
    v = SPEED_MAX * (2.0 * levels + 1.0 - VEL_N) / VEL_N
    w = np.exp(-0.5 * np.sum(v * v, axis=0)) / line_mean() ** 3
    modes = np.stack(
        [w, w * v[0], w * v[1], w * v[2]]
        + [0.5 * w * (v[d] * v[d] - 1.0) for d in range(3)]
        + [w * v[0] * v[1], w * v[0] * v[2], w * v[1] * v[2]]
    )
    weights = [np.ones_like(w)]
    for d in range(3):
        weights += [np.maximum(v[d], 0.0), np.minimum(v[d], 0.0)]
    return v, modes, np.stack(weights)


def line_mean():
    line = SPEED_MAX * (2.0 * np.arange(VEL_N) + 1.0 - VEL_N) / VEL_N
    return float(np.mean(np.exp(-0.5 * line * line)))


def constants(row_total):
    v, modes, weights = np_tables(row_total)
    gram = np.einsum("wv,mv,nv->wmn", weights, modes, modes)
    out = np.zeros((160, 16), np.float32)
    for w in range(7):
        out[16 * w : 16 * w + 10, :10] = gram[w]
    out[112, :10] = modes.sum(axis=1)
    for d in range(3):
        out[113 + d, :10] = modes @ v[d]
    first = [0, 1, 2, 3, 1, 2, 3, 1, 1, 2]
    second = [None, None, None, None, 1, 2, 3, 2, 3, 3]
    for r in range(10):
        out[120 + r, first[r]] = 1.0
        if second[r] is not None:
            out[136 + r, second[r]] = 1.0
    return out


def iota(shape, dim):
    return lax.broadcasted_iota(jnp.int32, shape, dim)


def eye():
    return (iota((RANK, RANK), 0) == iota((RANK, RANK), 1)).astype(F32)


def spread_lane(block, k):
    return jnp.broadcast_to(block[:, k : k + 1], (8, 128))


def spread_row(block, r):
    return jnp.broadcast_to(block[r : r + 1, :], (8, 128))


def chol_inverse(gram, width=4):
    lane = iota((8, 128), 1)
    sub = iota((8, 128), 0)
    on_diag = gram * eye()
    diag = jnp.sum(on_diag, axis=0, keepdims=True)
    row_scale = lax.rsqrt(diag)
    scaled = gram * row_scale * lax.rsqrt(jnp.sum(on_diag, axis=1, keepdims=True))
    wide = jnp.concatenate([scaled, jnp.zeros_like(gram)], axis=1)
    blocks = []
    for b in range(8):
        unit = jnp.where(lane == sub + (64 + 8 * b), 1.0, 0.0)
        blocks.append(wide[8 * b : 8 * b + 8] + unit)
    for k in range(0, RANK, width):
        b, r = divmod(k, 8)
        left = range(b, 8)
        cols = [{i: spread_lane(blocks[i], k + j) for i in left} for j in range(width)]
        heads = [spread_row(blocks[b], r + j) for j in range(width)]
        for j in range(0, width, 2):
            p = spread_row(cols[j][b], r + j)
            q = spread_row(cols[j][b], r + j + 1)
            s = spread_row(cols[j + 1][b], r + j + 1)
            inv_p = lax.rsqrt(p)
            both = inv_p * lax.rsqrt(p * s - q * q)
            pb, qb = both * p, both * q
            for i in left:
                first = cols[j][i]
                cols[j][i] = first * inv_p
                cols[j + 1][i] = pb * cols[j + 1][i] - qb * first
            first = heads[j]
            heads[j] = first * inv_p
            heads[j + 1] = pb * heads[j + 1] - qb * first
            for m in range(j + 2, width):
                u = spread_row(cols[j][b], r + m)
                w = spread_row(cols[j + 1][b], r + m)
                for i in left:
                    cols[m][i] = (cols[m][i] - cols[j][i] * u) - cols[j + 1][i] * w
                heads[m] = (heads[m] - heads[j] * u) - heads[j + 1] * w
        for i in left:
            if i == b and r + width == 8:
                new = blocks[i]
            else:
                new = blocks[i]
                for j in range(width):
                    new = new - cols[j][i] * heads[j]
            if i == b:
                new = jnp.where(sub >= r + width, new, blocks[i])
                for j in range(width):
                    new = jnp.where(sub == r + j, heads[j], new)
            blocks[i] = new
    full = jnp.concatenate(blocks, axis=0)
    keep = iota((RANK, RANK), 1) >= iota((RANK, RANK), 0)
    upper = jnp.where(keep, full[:, :RANK], 0.0) * (diag * row_scale)
    return upper, full[:, RANK:] * row_scale


def features(sel_map, field):
    both = mm(sel_map, field)
    lift = jnp.where(iota((16, field.shape[1]), 0) < 4, 1.0, 0.0)
    return both[:16] * (both[16:] + lift)


def pair_block(plus, minus):
    return jnp.where(iota((RANK, RANK), 0) <= iota((RANK, RANK), 1), plus, minus)


def weighted_payload(rows, v1, tab_ref, out_ref, stack_ref, scale, collide):
    modes = tab_ref[0:16, :]
    v2, v3 = tab_ref[18:19, :], tab_ref[19:20, :]
    weights = [None, jnp.maximum(v2, 0.0), jnp.minimum(v2, 0.0)]
    weights += [jnp.maximum(v3, 0.0), jnp.minimum(v3, 0.0)]
    for i in range(5):
        w = weights[i]
        stack_ref[80 * i : 80 * i + 64, :] = rows if w is None else rows * w
        stack_ref[80 * i + 64 : 80 * i + 80, :] = modes if w is None else modes * w
    stack_ref[400:408, :] = tab_ref[16:24, :]
    res = mmt(stack_ref[...], rows) * scale
    quads = [res[80 * i : 80 * i + 64] for i in range(5)]
    cross = [res[80 * i + 64 : 80 * i + 80] for i in range(5)]
    out_ref[...] = jnp.zeros_like(out_ref)
    out_ref[0:64, 0:64] = quads[0]
    out_ref[128:144, 0:64] = cross[0]
    if collide is not None:
        out_ref[136:152, 64:128] = collide
    v1p, v1m = jnp.maximum(v1, 0.0), jnp.minimum(v1, 0.0)
    pairs = [(quads[0] * v1p, quads[0] * v1m), (quads[1], quads[2]), (quads[3], quads[4])]
    crosses = [cross[0] * v1p, cross[0] * v1m] + cross[1:]
    out_ref[0:64, 64:128] = pair_block(*pairs[1])
    out_ref[64:128, 0:64] = pair_block(*pairs[0])
    out_ref[64:128, 64:128] = pair_block(*pairs[2])
    for i in range(6):
        out_ref[144 + 16 * i : 160 + 16 * i, 0:64] = crosses[i]
    out_ref[128:136, 64:128] = res[400:408]
    for d in range(3):
        diag = jnp.sum(pairs[d][1] * eye(), axis=0, keepdims=True)
        out_ref[152 + d : 153 + d, 64:128] = diag


def start_kernel(v1_ref, rows_ref, out_ref, tab_ref, stack_ref):
    v1 = v1_ref[0, 0]
    lanes = tab_ref.shape[1]
    at = iota((1, lanes), 1)
    v2 = SPEED_MAX * (2.0 * (at // VEL_N).astype(F32) + 1.0 - VEL_N) / VEL_N
    v3 = SPEED_MAX * (2.0 * (at % VEL_N).astype(F32) + 1.0 - VEL_N) / VEL_N
    v1 = jnp.full((1, lanes), v1, F32)
    w = jnp.exp(-0.5 * (v1 * v1 + v2 * v2 + v3 * v3)) / (line_mean() ** 3)
    tab_ref[...] = jnp.zeros_like(tab_ref)
    modes = [w, w * v1, w * v2, w * v3]
    modes += [0.5 * w * (v * v - 1.0) for v in (v1, v2, v3)]
    modes += [w * v1 * v2, w * v1 * v3, w * v2 * v3]
    for i, m in enumerate(modes):
        tab_ref[i : i + 1, :] = m
    for i, m in enumerate([jnp.ones_like(v1), v1, v2, v3]):
        tab_ref[16 + i : 17 + i, :] = m
    weighted_payload(rows_ref[...], v1_ref[0, 0], tab_ref, out_ref, stack_ref, 1.0, None)


def symmetric(sums, gain, cons):
    upper = iota((RANK, RANK), 0) <= iota((RANK, RANK), 1)
    diag = iota((RANK, RANK), 0) == iota((RANK, RANK), 1)
    packs = [sums[64:128, 0:64], sums[0:64, 64:128], sums[64:128, 64:128]]
    grams = [sums[0:64, 0:64]]
    for d in range(3):
        turned = packs[d].T
        grams.append(jnp.where(upper, packs[d], turned))
        grams.append(
            jnp.where(diag, sums[152 + d : 153 + d, 64:128], jnp.where(upper, turned, packs[d]))
        )
    mode_gain = mmt(cons[0:120], gain)
    for w in range(7):
        half = sums[128 + 16 * w : 144 + 16 * w, 0:64] + 0.5 * mode_gain[16 * w : 16 * w + 16]
        cross = mm(gain, half)
        grams[w] = grams[w] + (cross + cross.T)
    mode_rows = sums[128:144, 0:64] + mode_gain[0:16]
    moments = sums[128:136, 64:128] + mode_gain[112:120]
    return grams, mode_rows, moments


def shifted_stack(p, stack_ref, mine, lower, upper, yl_ref, yh_ref, zl_ref, zh_ref):
    lane = iota((RANK, 128), 1)
    field = mine[...]
    stack_ref[0:64, :] = field
    stack_ref[64:128, :] = lower[...]
    stack_ref[256:320, :] = upper[...]
    n = field.shape[1] // 128
    zl, zh = zl_ref[...], zh_ref[...]
    for y in range(n):
        here = field[:, 128 * y : 128 * y + 128]
        cols = slice(128 * y, 128 * y + 128)
        halo = slice(128 * p, 128 * p + 128)
        stack_ref[128:192, cols] = yl_ref[:, halo] if y == 0 else field[:, 128 * (y - 1) : 128 * y]
        stack_ref[320:384, cols] = (
            yh_ref[:, halo] if y == n - 1 else field[:, 128 * (y + 1) : 128 * (y + 2)]
        )
        g = p * n + y
        low = pltpu.roll(zl, (128 - g) % 128, 1)
        stack_ref[192:256, cols] = jnp.where(lane == 0, low, pltpu.roll(here, 1, 1))
        high = pltpu.roll(zh, 127 - g, 1)
        stack_ref[384:448, cols] = jnp.where(lane == 127, high, pltpu.roll(here, 127, 1))


def maps_kernel(
    count, cells, sums_ref, base_ref, cons_ref, fa, fb, xh, yl, yh, zl, zh,
    kb_ref, map_ref, sel_ref, seln_ref, gw_ref, mode_ref, mom_ref, civ_ref, ginv_ref, gain_ref,
    stack_ref,
):
    sums, base, cons = sums_ref[...], base_ref[...], cons_ref[...]
    gain = (TIME_STEP / cells) * mmt(base, sums[136:152, 64:128])
    gain_ref[...] = gain
    grams, mode_rows, moments = symmetric(sums, gain, cons)
    shifted_stack(1, stack_ref, fb, fa, xh, yl, yh, zl, zh)
    sides = mm(jnp.concatenate(grams, axis=0), base)
    sides = [sides[64 * w : 64 * w + 64] for w in range(7)]
    stay = (1.0 - TIME_STEP) * sides[0]
    for d in range(3):
        stay = stay + TIME_STEP * (sides[2 * d + 2] - sides[2 * d + 1])
    row = [stay] + [TIME_STEP * sides[2 * d + 1] for d in range(3)]
    row += [-TIME_STEP * sides[2 * d + 2] for d in range(3)] + [TIME_STEP * mode_rows.T]
    row = jnp.concatenate(row, axis=1) * (1.0 / count)
    sel = mm(cons[120:152, 0:8], mm(moments, base) * (1.0 / count))
    sel_ref[...] = sel
    stack_ref[448:464, :] = features(sel, fb[...])
    gw_ref[...] = jnp.concatenate(grams[1:], axis=1)
    mode_ref[...] = mode_rows
    mom_ref[...] = moments
    _, civ = chol_inverse(grams[0] * (1.0 / count))
    maps = mm(civ, row)
    kb_ref[...] = mm(maps, stack_ref[...])
    map_ref[...] = maps
    civ_ref[...] = civ
    ginv_ref[...] = mm(civ.T, civ) * (1.0 / count)
    seln_ref[...] = mm(cons[120:152, 0:8], mmt(moments, civ) * (1.0 / count))


def columns(fields, lane_at):
    lane = iota((RANK, 128), 1)
    out = jnp.zeros((RANK, 128), F32)
    g = 0
    for field in fields:
        for y in range(field.shape[1] // 128):
            here = field[:, 128 * y : 128 * y + 128]
            out = jnp.where(lane == g, pltpu.roll(here, (g - lane_at) % 128, 1), out)
            g += 1
    return out


def plane_kernel(
    map_ref, sel_ref, fa, fb, xl, yl, yh, zl, zh, kb,
    ka_ref, ylo_ref, yho_ref, zlo_ref, zho_ref, stack_ref,
):
    shifted_stack(0, stack_ref, fa, xl, fb, yl, yh, zl, zh)
    stack_ref[448:464, :] = features(sel_ref[...], fa[...])
    ka = mm(map_ref[...], stack_ref[...])
    ka_ref[...] = ka
    kb = kb[...]
    n = ka.shape[1]
    ylo_ref[...] = jnp.concatenate([ka[:, n - 128 :], kb[:, n - 128 :]], axis=1)
    yho_ref[...] = jnp.concatenate([ka[:, :128], kb[:, :128]], axis=1)
    zlo_ref[...] = columns((ka, kb), 127)
    zho_ref[...] = columns((ka, kb), 0)


def inner_kernel(seln_ref, ka, kb, out_ref, stack_ref):
    lane = iota((RANK, 128), 1)
    n = ka.shape[1]
    zero = jnp.zeros((RANK, 128), F32)
    for p, ref in enumerate((ka, kb)):
        at = p * n
        field = ref[...]
        stack_ref[0:64, at : at + n] = field
        stack_ref[128:192, at : at + 128] = zero
        stack_ref[128:192, at + 128 : at + n] = field[:, : n - 128]
        for y in range(n // 128):
            here = field[:, 128 * y : 128 * y + 128]
            stack_ref[192:256, at + 128 * y : at + 128 * y + 128] = jnp.where(
                lane == 0, 0.0, pltpu.roll(here, 1, 1)
            )
        stack_ref[256:272, at : at + n] = features(seln_ref[...], field)
    stack_ref[64:128, 0:n] = jnp.zeros((RANK, n), F32)
    stack_ref[64:128, n : 2 * n] = ka[...]
    out_ref[...] = mmt(stack_ref[...], stack_ref[0:64, :])


def edge_kernel(part_ref, ka, xl, yl, yh, zl, zh, out_ref):
    part = part_ref[...]
    out_ref[0:64, 0:64] = part[0:64]
    out_ref[32:48, 0:32] = part[256:272, 0:32]
    out_ref[48:64, 0:32] = part[256:272, 32:64]
    out_ref[0:64, 64:128] = part[64:128] + mmt(xl[...], ka[...])
    out_ref[64:128, 0:64] = part[128:192] + mmt(yl[...], yh[...])
    out_ref[64:128, 64:128] = part[192:256] + mmt(zl[...], zh[...])


def core_kernel(
    count, cells, nz, v1_ref, sums_ref, ka, kb, rows_ref, gain_ref, tab_ref, cons_ref,
    gw_ref, mode_ref, mom_ref, civ_ref, ginv_ref, out_ref, rows_out, cxi_ref, stack_ref, base_ref,
):
    v1 = v1_ref[0, 0]
    rows = rows_ref[...] + mm(gain_ref[...], tab_ref[0:16, :])
    v2, v3 = tab_ref[18:19, :], tab_ref[19:20, :]
    base_ref[0:64, :] = rows
    base_ref[64:128, :] = rows * jnp.maximum(v2, 0.0)
    base_ref[128:192, :] = rows * jnp.minimum(v2, 0.0)
    base_ref[192:256, :] = rows * jnp.maximum(v3, 0.0)
    base_ref[256:320, :] = rows * jnp.minimum(v3, 0.0)
    sums = sums_ref[...] * (1.0 / cells)
    civ = civ_ref[...]
    unit = eye()
    gram = sums[0:64, 0:64]
    corner = (iota((RANK, RANK), 0) >= 32) & (iota((RANK, RANK), 1) < 32)
    up, cxi = chol_inverse(jnp.where(corner, gram.T, gram))
    cxi_ref[...] = cxi
    moment_x = jnp.concatenate([sums[32:48, 0:32], sums[48:64, 0:32]], axis=1)
    y = mm(up, civ)
    zs = jnp.concatenate([sums[0:64, 64:128], sums[64:128, 0:64], sums[64:128, 64:128]], axis=0)
    zs = mmt(zs, cxi)
    lower, upper = [], []
    for d in range(3):
        turned = mm(cxi, zs[64 * d : 64 * d + 64])
        lower.append(unit - turned.T)
        upper.append(turned - unit)
    yg = mm(y, gw_ref[...])
    yg = jnp.concatenate([yg[:, 64 * w : 64 * w + 64] for w in range(6)], axis=0)
    sides = jnp.concatenate([lower[0], upper[0], lower[1], upper[1], lower[2], upper[2]], axis=1)
    rate = mm(mmt(cxi, moment_x), mode_ref[...]) - mm(sides, yg)
    y = (1.0 + TIME_STEP) * y - TIME_STEP * mm(rate, ginv_ref[...])
    sel = mm(cons_ref[120:152, 0:8], mm(mmt(mom_ref[...], y) * (1.0 / count), cxi))
    collide = mmt(features(sel, ka[...]), ka[...]) + mmt(features(sel, kb[...]), kb[...])
    turn = lower[0] * jnp.maximum(v1, 0.0) + upper[0] * jnp.minimum(v1, 0.0)
    move = [(1.0 - TIME_STEP) * unit - TIME_STEP * turn]
    move += [-TIME_STEP * m for m in (lower[1], upper[1], lower[2], upper[2])]
    move = mm(jnp.concatenate(move, axis=0), y)
    move = jnp.concatenate([move[64 * t : 64 * t + 64] for t in range(5)], axis=1)
    rows = mm(move, base_ref[...])
    rows_out[...] = rows
    weighted_payload(rows, v1, tab_ref, out_ref, stack_ref, 1.0 / nz, collide)


def space_kernel(cxi_ref, ka, kb, out_ref):
    for p, ref in enumerate((ka, kb)):
        field = mm(cxi_ref[...], ref[...])
        for y in range(out_ref.shape[2]):
            out_ref[:, p, y, :] = field[:, 128 * y : 128 * y + 128]


def finish_kernel(count, cells, sums_ref, cxi_ref, rows_ref, tab_ref, cons_ref, low_ref, out_ref):
    sums = sums_ref[...]
    gain = (TIME_STEP / cells) * mmt(cxi_ref[...], sums[136:152, 64:128])
    half = sums[128:144, 0:64] + 0.5 * mmt(cons_ref[0:16, :], gain)
    cross = mm(gain, half)
    up, civ = chol_inverse((sums[0:64, 0:64] + (cross + cross.T)) * (1.0 / count))
    low_ref[...] = up.T
    out_ref[...] = mm(civ, rows_ref[...] + mm(gain, tab_ref[0:16, :]))


def call(kernel, outs, scratch, *args):
    shapes = [jax.ShapeDtypeStruct(s, F32) for s in outs]
    specs = [pl.BlockSpec(memory_space=pltpu.VMEM) for _ in args]
    if args[0].shape == (1, 1):
        specs[0] = pl.BlockSpec(memory_space=pltpu.SMEM)
    return pl.pallas_call(
        kernel,
        out_shape=shapes,
        in_specs=specs,
        out_specs=[pl.BlockSpec(memory_space=pltpu.VMEM) for _ in outs],
        scratch_shapes=[pltpu.VMEM(s, F32) for s in scratch],
        compiler_params=pltpu.CompilerParams(vmem_limit_bytes=40 * 1024 * 1024),
    )(*args)


def route(axis, step):
    n = lax.axis_size(axis)
    return [(i, (i + step) % n) for i in range(n)]


def swap(chunks, axis):
    return lax.all_to_all(chunks, axis, 0, 0, tiled=True)


def spread(part, n):
    return jnp.broadcast_to(part[None], (n,) + part.shape)


def plane_sum(payload):
    n = lax.axis_size(PLANE)
    return jnp.sum(swap(payload.reshape(n, -1, 128), PLANE), axis=0)


def line_sum(part):
    return jnp.sum(swap(spread(part, lax.axis_size("bz")), "bz"), axis=0)


def plane_gather(part):
    return swap(spread(part, lax.axis_size(PLANE)), PLANE).reshape(-1, 128)


def local(space_factor, core_matrix, velocity_factor):
    vel_rows = velocity_factor.shape[1]
    plane = lax.axis_index(PLANE)
    count = vel_rows * lax.axis_size(PLANE)
    nz = lax.axis_size("bz")
    shape = space_factor.shape
    half = shape[2] * shape[3]
    cells = 2 * half * lax.axis_size(PLANE) * nz
    cons = jnp.asarray(constants(count))
    digit = (plane * vel_rows) // (VEL_N * VEL_N)
    v1 = SPEED_MAX * (2.0 * digit.astype(F32) + 1.0 - VEL_N) / VEL_N
    v1 = v1.reshape(1, 1)

    fa = space_factor[:, 0].reshape(RANK, half)
    fb = space_factor[:, 1].reshape(RANK, half)
    payload, tab = call(
        start_kernel, [(256, 128), (24, vel_rows)], [(408, vel_rows)], v1, velocity_factor
    )
    yl = space_factor[:, :, -1].reshape(RANK, 256)
    yh = space_factor[:, :, 0].reshape(RANK, 256)
    pad = jnp.zeros((RANK, 128 - 2 * shape[2]), F32)
    zl = jnp.concatenate([space_factor[:, :, :, -1].reshape(RANK, -1), pad], axis=1)
    zh = jnp.concatenate([space_factor[:, :, :, 0].reshape(RANK, -1), pad], axis=1)

    def halo(planes, step):
        out = []
        for field, axis in zip(planes, ("bx", "by", "bz")):
            out.append(lax.ppermute(field, axis, route(axis, step)))
        return tuple(out)

    def low_halo(*planes):
        return halo(planes, 1)

    def high_halo(*planes):
        return halo(planes, -1)

    low = low_halo(fb, yl, zl)
    high = high_halo(fa, yh, zh)
    part = plane_sum(payload)
    sums = plane_gather(part)

    def step(turn, carry):
        fa, fb, low, high, sums, rows, base, _ = carry
        kb, maps, sel, seln, gw, mode_rows, moments, civ, ginv, gain = call(
            functools.partial(maps_kernel, count, cells),
            [(RANK, half), (RANK, 464), (32, RANK), (32, RANK), (RANK, 384), (16, RANK), (8, RANK),
             (RANK, RANK), (RANK, RANK), (RANK, 16)],
            [(464, half)],
            sums, base, cons, fa, fb, high[0], low[1], high[1], low[2], high[2],
        )
        ka, yl, yh, zl, zh = call(
            plane_kernel,
            [(RANK, half), (RANK, 256), (RANK, 256), (RANK, 128), (RANK, 128)],
            [(464, half)],
            maps, sel, fa, fb, low[0], low[1], high[1], low[2], high[2], kb,
        )
        low = low_halo(kb, yl, zl)
        (part,) = call(inner_kernel, [(272, RANK)], [(272, 2 * half)], seln, ka, kb)
        (payload,) = call(edge_kernel, [(128, 128)], [], part, ka, low[0], low[1], yh, low[2], zh)
        high = high_halo(ka, yh, zh)
        sums = plane_gather(line_sum(plane_sum(payload)))
        payload, rows, base = call(
            functools.partial(core_kernel, count, cells, nz),
            [(256, 128), (RANK, vel_rows), (RANK, RANK)],
            [(408, vel_rows), (320, vel_rows)],
            v1, sums, ka, kb, rows, gain, tab, cons, gw, mode_rows, moments, civ, ginv,
        )
        (space,) = call(space_kernel, [shape], [], base, ka, kb)
        sums = plane_gather(line_sum(plane_sum(payload)))
        return ka, kb, low, high, sums, rows, base, space

    carry = (fa, fb, low, high, sums, velocity_factor, core_matrix.T, jnp.zeros(shape, F32))
    _, _, _, _, sums, rows, base, new_space = lax.fori_loop(0, STEPS, step, carry)
    new_core, new_velocity = call(
        functools.partial(finish_kernel, count, cells),
        [(RANK, RANK), (RANK, vel_rows)], [], sums, base, rows, tab, cons,
    )
    return new_space, new_core, new_velocity


def solution(mesh):
    return jax.shard_map(
        local,
        mesh=mesh,
        in_specs=(P(None, "bx", "by", "bz"), P(), P(None, PLANE)),
        out_specs=(P(None, "bx", "by", "bz"), P(), P(None, PLANE)),
        check_vma=False,
    )
```

```python
import functools

import jax
import jax.numpy as jnp
import numpy as np
from jax import lax
from jax.experimental import pallas as pl
from jax.experimental.pallas import tpu as pltpu
from jax.sharding import PartitionSpec as P


VEL_N = 32
STEPS = 2
TIME_STEP = 0.1
SPEED_MAX = 3.0
HIGHEST = lax.Precision.HIGHEST
PLANE = ("bx", "by")
RANK = 64
F32 = jnp.float32


def mm(a, b):
    return jnp.dot(a, b, precision=HIGHEST, preferred_element_type=F32)


def mmt(a, b):
    return lax.dot_general(
        a, b, (((1,), (1,)), ((), ())), precision=HIGHEST, preferred_element_type=F32
    )


def np_tables(row_total):
    row_ids = np.arange(row_total)
    levels = np.stack([row_ids // (VEL_N * VEL_N), row_ids // VEL_N % VEL_N, row_ids % VEL_N])
    v = SPEED_MAX * (2.0 * levels + 1.0 - VEL_N) / VEL_N
    w = np.exp(-0.5 * np.sum(v * v, axis=0)) / line_mean() ** 3
    modes = np.stack(
        [w, w * v[0], w * v[1], w * v[2]]
        + [0.5 * w * (v[d] * v[d] - 1.0) for d in range(3)]
        + [w * v[0] * v[1], w * v[0] * v[2], w * v[1] * v[2]]
    )
    weights = [np.ones_like(w)]
    for d in range(3):
        weights += [np.maximum(v[d], 0.0), np.minimum(v[d], 0.0)]
    return v, modes, np.stack(weights)


def line_mean():
    line = SPEED_MAX * (2.0 * np.arange(VEL_N) + 1.0 - VEL_N) / VEL_N
    return float(np.mean(np.exp(-0.5 * line * line)))


def constants(row_total):
    v, modes, weights = np_tables(row_total)
    gram = np.einsum("wv,mv,nv->wmn", weights, modes, modes)
    out = np.zeros((160, 16), np.float32)
    for w in range(7):
        out[16 * w : 16 * w + 10, :10] = gram[w]
    out[112, :10] = modes.sum(axis=1)
    for d in range(3):
        out[113 + d, :10] = modes @ v[d]
    first = [0, 1, 2, 3, 1, 2, 3, 1, 1, 2]
    second = [None, None, None, None, 1, 2, 3, 2, 3, 3]
    for r in range(10):
        out[120 + r, first[r]] = 1.0
        if second[r] is not None:
            out[136 + r, second[r]] = 1.0
    return out


def iota(shape, dim):
    return lax.broadcasted_iota(jnp.int32, shape, dim)


def eye():
    return (iota((RANK, RANK), 0) == iota((RANK, RANK), 1)).astype(F32)


def spread_lane(block, k):
    return jnp.broadcast_to(block[:, k : k + 1], (8, 128))


def spread_row(block, r):
    return jnp.broadcast_to(block[r : r + 1, :], (8, 128))


def chol_inverse(gram, width=4):
    lane = iota((8, 128), 1)
    sub = iota((8, 128), 0)
    on_diag = gram * eye()
    diag = jnp.sum(on_diag, axis=0, keepdims=True)
    row_scale = lax.rsqrt(diag)
    scaled = gram * row_scale * lax.rsqrt(jnp.sum(on_diag, axis=1, keepdims=True))
    wide = jnp.concatenate([scaled, jnp.zeros_like(gram)], axis=1)
    blocks = []
    for b in range(8):
        unit = jnp.where(lane == sub + (64 + 8 * b), 1.0, 0.0)
        blocks.append(wide[8 * b : 8 * b + 8] + unit)
    for k in range(0, RANK, width):
        b, r = divmod(k, 8)
        left = range(b, 8)
        cols = [{i: spread_lane(blocks[i], k + j) for i in left} for j in range(width)]
        heads = [spread_row(blocks[b], r + j) for j in range(width)]
        for j in range(0, width, 2):
            p = spread_row(cols[j][b], r + j)
            q = spread_row(cols[j][b], r + j + 1)
            s = spread_row(cols[j + 1][b], r + j + 1)
            inv_p = lax.rsqrt(p)
            both = inv_p * lax.rsqrt(p * s - q * q)
            pb, qb = both * p, both * q
            for i in left:
                first = cols[j][i]
                cols[j][i] = first * inv_p
                cols[j + 1][i] = pb * cols[j + 1][i] - qb * first
            first = heads[j]
            heads[j] = first * inv_p
            heads[j + 1] = pb * heads[j + 1] - qb * first
            for m in range(j + 2, width):
                u = spread_row(cols[j][b], r + m)
                w = spread_row(cols[j + 1][b], r + m)
                for i in left:
                    cols[m][i] = (cols[m][i] - cols[j][i] * u) - cols[j + 1][i] * w
                heads[m] = (heads[m] - heads[j] * u) - heads[j + 1] * w
        for i in left:
            if i == b and r + width == 8:
                new = blocks[i]
            else:
                new = blocks[i]
                for j in range(width):
                    new = new - cols[j][i] * heads[j]
            if i == b:
                new = jnp.where(sub >= r + width, new, blocks[i])
                for j in range(width):
                    new = jnp.where(sub == r + j, heads[j], new)
            blocks[i] = new
    full = jnp.concatenate(blocks, axis=0)
    keep = iota((RANK, RANK), 1) >= iota((RANK, RANK), 0)
    upper = jnp.where(keep, full[:, :RANK], 0.0) * (diag * row_scale)
    return upper, full[:, RANK:] * row_scale


def features(sel_map, field):
    both = mm(sel_map, field)
    lift = jnp.where(iota((16, field.shape[1]), 0) < 4, 1.0, 0.0)
    return both[:16] * (both[16:] + lift)


def pair_block(plus, minus):
    return jnp.where(iota((RANK, RANK), 0) <= iota((RANK, RANK), 1), plus, minus)


def weighted_payload(rows, v1, tab_ref, out_ref, stack_ref, scale, collide):
    modes = tab_ref[0:16, :]
    v2, v3 = tab_ref[18:19, :], tab_ref[19:20, :]
    weights = [None, jnp.maximum(v2, 0.0), jnp.minimum(v2, 0.0)]
    weights += [jnp.maximum(v3, 0.0), jnp.minimum(v3, 0.0)]
    for i in range(5):
        w = weights[i]
        stack_ref[80 * i : 80 * i + 64, :] = rows if w is None else rows * w
        stack_ref[80 * i + 64 : 80 * i + 80, :] = modes if w is None else modes * w
    stack_ref[400:408, :] = tab_ref[16:24, :]
    res = mmt(stack_ref[...], rows) * scale
    quads = [res[80 * i : 80 * i + 64] for i in range(5)]
    cross = [res[80 * i + 64 : 80 * i + 80] for i in range(5)]
    out_ref[...] = jnp.zeros_like(out_ref)
    out_ref[0:64, 0:64] = quads[0]
    out_ref[128:144, 0:64] = cross[0]
    if collide is not None:
        out_ref[136:152, 64:128] = collide
    v1p, v1m = jnp.maximum(v1, 0.0), jnp.minimum(v1, 0.0)
    pairs = [(quads[0] * v1p, quads[0] * v1m), (quads[1], quads[2]), (quads[3], quads[4])]
    crosses = [cross[0] * v1p, cross[0] * v1m] + cross[1:]
    out_ref[0:64, 64:128] = pair_block(*pairs[1])
    out_ref[64:128, 0:64] = pair_block(*pairs[0])
    out_ref[64:128, 64:128] = pair_block(*pairs[2])
    for i in range(6):
        out_ref[144 + 16 * i : 160 + 16 * i, 0:64] = crosses[i]
    out_ref[128:136, 64:128] = res[400:408]
    for d in range(3):
        diag = jnp.sum(pairs[d][1] * eye(), axis=0, keepdims=True)
        out_ref[152 + d : 153 + d, 64:128] = diag


def start_kernel(v1_ref, rows_ref, out_ref, tab_ref, stack_ref):
    v1 = v1_ref[0, 0]
    lanes = tab_ref.shape[1]
    at = iota((1, lanes), 1)
    v2 = SPEED_MAX * (2.0 * (at // VEL_N).astype(F32) + 1.0 - VEL_N) / VEL_N
    v3 = SPEED_MAX * (2.0 * (at % VEL_N).astype(F32) + 1.0 - VEL_N) / VEL_N
    v1 = jnp.full((1, lanes), v1, F32)
    w = jnp.exp(-0.5 * (v1 * v1 + v2 * v2 + v3 * v3)) / (line_mean() ** 3)
    tab_ref[...] = jnp.zeros_like(tab_ref)
    modes = [w, w * v1, w * v2, w * v3]
    modes += [0.5 * w * (v * v - 1.0) for v in (v1, v2, v3)]
    modes += [w * v1 * v2, w * v1 * v3, w * v2 * v3]
    for i, m in enumerate(modes):
        tab_ref[i : i + 1, :] = m
    for i, m in enumerate([jnp.ones_like(v1), v1, v2, v3]):
        tab_ref[16 + i : 17 + i, :] = m
    weighted_payload(rows_ref[...], v1_ref[0, 0], tab_ref, out_ref, stack_ref, 1.0, None)


def symmetric(sums, gain, cons):
    upper = iota((RANK, RANK), 0) <= iota((RANK, RANK), 1)
    diag = iota((RANK, RANK), 0) == iota((RANK, RANK), 1)
    packs = [sums[64:128, 0:64], sums[0:64, 64:128], sums[64:128, 64:128]]
    grams = [sums[0:64, 0:64]]
    for d in range(3):
        turned = packs[d].T
        grams.append(jnp.where(upper, packs[d], turned))
        grams.append(
            jnp.where(diag, sums[152 + d : 153 + d, 64:128], jnp.where(upper, turned, packs[d]))
        )
    mode_gain = mmt(cons[0:120], gain)
    for w in range(7):
        half = sums[128 + 16 * w : 144 + 16 * w, 0:64] + 0.5 * mode_gain[16 * w : 16 * w + 16]
        cross = mm(gain, half)
        grams[w] = grams[w] + (cross + cross.T)
    mode_rows = sums[128:144, 0:64] + mode_gain[0:16]
    moments = sums[128:136, 64:128] + mode_gain[112:120]
    return grams, mode_rows, moments


def shifted_stack(p, stack_ref, mine, lower, upper, yl_ref, yh_ref, zl_ref, zh_ref):
    lane = iota((RANK, 128), 1)
    field = mine[...]
    stack_ref[0:64, :] = field
    stack_ref[64:128, :] = lower[...]
    stack_ref[256:320, :] = upper[...]
    n = field.shape[1] // 128
    zl, zh = zl_ref[...], zh_ref[...]
    for y in range(n):
        here = field[:, 128 * y : 128 * y + 128]
        cols = slice(128 * y, 128 * y + 128)
        halo = slice(128 * p, 128 * p + 128)
        stack_ref[128:192, cols] = yl_ref[:, halo] if y == 0 else field[:, 128 * (y - 1) : 128 * y]
        stack_ref[320:384, cols] = (
            yh_ref[:, halo] if y == n - 1 else field[:, 128 * (y + 1) : 128 * (y + 2)]
        )
        g = p * n + y
        low = pltpu.roll(zl, (128 - g) % 128, 1)
        stack_ref[192:256, cols] = jnp.where(lane == 0, low, pltpu.roll(here, 1, 1))
        high = pltpu.roll(zh, 127 - g, 1)
        stack_ref[384:448, cols] = jnp.where(lane == 127, high, pltpu.roll(here, 127, 1))


def maps_kernel(
    count, cells, sums_ref, base_ref, cons_ref, fa, fb, xh, yl, yh, zl, zh,
    kb_ref, map_ref, sel_ref, seln_ref, gw_ref, mode_ref, mom_ref, civ_ref, ginv_ref, gain_ref,
    stack_ref,
):
    sums, base, cons = sums_ref[...], base_ref[...], cons_ref[...]
    gain = (TIME_STEP / cells) * mmt(base, sums[136:152, 64:128])
    gain_ref[...] = gain
    grams, mode_rows, moments = symmetric(sums, gain, cons)
    shifted_stack(1, stack_ref, fb, fa, xh, yl, yh, zl, zh)
    sides = mm(jnp.concatenate(grams, axis=0), base)
    sides = [sides[64 * w : 64 * w + 64] for w in range(7)]
    stay = (1.0 - TIME_STEP) * sides[0]
    for d in range(3):
        stay = stay + TIME_STEP * (sides[2 * d + 2] - sides[2 * d + 1])
    row = [stay] + [TIME_STEP * sides[2 * d + 1] for d in range(3)]
    row += [-TIME_STEP * sides[2 * d + 2] for d in range(3)] + [TIME_STEP * mode_rows.T]
    row = jnp.concatenate(row, axis=1) * (1.0 / count)
    sel = mm(cons[120:152, 0:8], mm(moments, base) * (1.0 / count))
    sel_ref[...] = sel
    stack_ref[448:464, :] = features(sel, fb[...])
    gw_ref[...] = jnp.concatenate(grams[1:], axis=1)
    mode_ref[...] = mode_rows
    mom_ref[...] = moments
    _, civ = chol_inverse(grams[0] * (1.0 / count))
    maps = mm(civ, row)
    kb_ref[...] = mm(maps, stack_ref[...])
    map_ref[...] = maps
    civ_ref[...] = civ
    ginv_ref[...] = mm(civ.T, civ) * (1.0 / count)
    seln_ref[...] = mm(cons[120:152, 0:8], mmt(moments, civ) * (1.0 / count))


def columns(fields, lane_at):
    lane = iota((RANK, 128), 1)
    out = jnp.zeros((RANK, 128), F32)
    g = 0
    for field in fields:
        for y in range(field.shape[1] // 128):
            here = field[:, 128 * y : 128 * y + 128]
            out = jnp.where(lane == g, pltpu.roll(here, (g - lane_at) % 128, 1), out)
            g += 1
    return out


def plane_kernel(
    map_ref, sel_ref, fa, fb, xl, yl, yh, zl, zh, kb,
    ka_ref, ylo_ref, yho_ref, zlo_ref, zho_ref, stack_ref,
):
    shifted_stack(0, stack_ref, fa, xl, fb, yl, yh, zl, zh)
    stack_ref[448:464, :] = features(sel_ref[...], fa[...])
    ka = mm(map_ref[...], stack_ref[...])
    ka_ref[...] = ka
    kb = kb[...]
    n = ka.shape[1]
    ylo_ref[...] = jnp.concatenate([ka[:, n - 128 :], kb[:, n - 128 :]], axis=1)
    yho_ref[...] = jnp.concatenate([ka[:, :128], kb[:, :128]], axis=1)
    zlo_ref[...] = columns((ka, kb), 127)
    zho_ref[...] = columns((ka, kb), 0)


def inner_kernel(seln_ref, ka, kb, out_ref, stack_ref):
    lane = iota((RANK, 128), 1)
    n = ka.shape[1]
    zero = jnp.zeros((RANK, 128), F32)
    for p, ref in enumerate((ka, kb)):
        at = p * n
        field = ref[...]
        stack_ref[0:64, at : at + n] = field
        stack_ref[128:192, at : at + 128] = zero
        stack_ref[128:192, at + 128 : at + n] = field[:, : n - 128]
        for y in range(n // 128):
            here = field[:, 128 * y : 128 * y + 128]
            stack_ref[192:256, at + 128 * y : at + 128 * y + 128] = jnp.where(
                lane == 0, 0.0, pltpu.roll(here, 1, 1)
            )
        stack_ref[256:272, at : at + n] = features(seln_ref[...], field)
    stack_ref[64:128, 0:n] = jnp.zeros((RANK, n), F32)
    stack_ref[64:128, n : 2 * n] = ka[...]
    out_ref[...] = mmt(stack_ref[...], stack_ref[0:64, :])


def edge_kernel(part_ref, ka, xl, yl, yh, zl, zh, out_ref):
    part = part_ref[...]
    out_ref[0:64, 0:64] = part[0:64]
    out_ref[32:48, 0:32] = part[256:272, 0:32]
    out_ref[48:64, 0:32] = part[256:272, 32:64]
    out_ref[0:64, 64:128] = part[64:128] + mmt(xl[...], ka[...])
    out_ref[64:128, 0:64] = part[128:192] + mmt(yl[...], yh[...])
    out_ref[64:128, 64:128] = part[192:256] + mmt(zl[...], zh[...])


def core_kernel(
    count, cells, nz, v1_ref, sums_ref, ka, kb, rows_ref, gain_ref, tab_ref, cons_ref,
    gw_ref, mode_ref, mom_ref, civ_ref, ginv_ref, out_ref, rows_out, cxi_ref, stack_ref, base_ref,
):
    v1 = v1_ref[0, 0]
    rows = rows_ref[...] + mm(gain_ref[...], tab_ref[0:16, :])
    v2, v3 = tab_ref[18:19, :], tab_ref[19:20, :]
    base_ref[0:64, :] = rows
    base_ref[64:128, :] = rows * jnp.maximum(v2, 0.0)
    base_ref[128:192, :] = rows * jnp.minimum(v2, 0.0)
    base_ref[192:256, :] = rows * jnp.maximum(v3, 0.0)
    base_ref[256:320, :] = rows * jnp.minimum(v3, 0.0)
    sums = sums_ref[...] * (1.0 / cells)
    civ = civ_ref[...]
    unit = eye()
    gram = sums[0:64, 0:64]
    corner = (iota((RANK, RANK), 0) >= 32) & (iota((RANK, RANK), 1) < 32)
    up, cxi = chol_inverse(jnp.where(corner, gram.T, gram))
    cxi_ref[...] = cxi
    moment_x = jnp.concatenate([sums[32:48, 0:32], sums[48:64, 0:32]], axis=1)
    y = mm(up, civ)
    zs = jnp.concatenate([sums[0:64, 64:128], sums[64:128, 0:64], sums[64:128, 64:128]], axis=0)
    zs = mmt(zs, cxi)
    lower, upper = [], []
    for d in range(3):
        turned = mm(cxi, zs[64 * d : 64 * d + 64])
        lower.append(unit - turned.T)
        upper.append(turned - unit)
    yg = mm(y, gw_ref[...])
    yg = jnp.concatenate([yg[:, 64 * w : 64 * w + 64] for w in range(6)], axis=0)
    sides = jnp.concatenate([lower[0], upper[0], lower[1], upper[1], lower[2], upper[2]], axis=1)
    rate = mm(mmt(cxi, moment_x), mode_ref[...]) - mm(sides, yg)
    y = (1.0 + TIME_STEP) * y - TIME_STEP * mm(rate, ginv_ref[...])
    sel = mm(cons_ref[120:152, 0:8], mm(mmt(mom_ref[...], y) * (1.0 / count), cxi))
    collide = mmt(features(sel, ka[...]), ka[...]) + mmt(features(sel, kb[...]), kb[...])
    turn = lower[0] * jnp.maximum(v1, 0.0) + upper[0] * jnp.minimum(v1, 0.0)
    move = [(1.0 - TIME_STEP) * unit - TIME_STEP * turn]
    move += [-TIME_STEP * m for m in (lower[1], upper[1], lower[2], upper[2])]
    move = mm(jnp.concatenate(move, axis=0), y)
    move = jnp.concatenate([move[64 * t : 64 * t + 64] for t in range(5)], axis=1)
    rows = mm(move, base_ref[...])
    rows_out[...] = rows
    weighted_payload(rows, v1, tab_ref, out_ref, stack_ref, 1.0 / nz, collide)


def space_kernel(cxi_ref, ka, kb, out_ref):
    for p, ref in enumerate((ka, kb)):
        field = mm(cxi_ref[...], ref[...])
        for y in range(out_ref.shape[2]):
            out_ref[:, p, y, :] = field[:, 128 * y : 128 * y + 128]


def finish_kernel(count, cells, sums_ref, cxi_ref, rows_ref, tab_ref, cons_ref, low_ref, out_ref):
    sums = sums_ref[...]
    gain = (TIME_STEP / cells) * mmt(cxi_ref[...], sums[136:152, 64:128])
    half = sums[128:144, 0:64] + 0.5 * mmt(cons_ref[0:16, :], gain)
    cross = mm(gain, half)
    up, civ = chol_inverse((sums[0:64, 0:64] + (cross + cross.T)) * (1.0 / count))
    low_ref[...] = up.T
    out_ref[...] = mm(civ, rows_ref[...] + mm(gain, tab_ref[0:16, :]))


def call(kernel, outs, scratch, *args, alias=None):
    shapes = [jax.ShapeDtypeStruct(s, F32) for s in outs]
    specs = [pl.BlockSpec(memory_space=pltpu.VMEM) for _ in args]
    if args[0].shape == (1, 1):
        specs[0] = pl.BlockSpec(memory_space=pltpu.SMEM)
    return pl.pallas_call(
        kernel,
        out_shape=shapes,
        in_specs=specs,
        out_specs=[pl.BlockSpec(memory_space=pltpu.VMEM) for _ in outs],
        scratch_shapes=[pltpu.VMEM(s, F32) for s in scratch],
        input_output_aliases=alias or {},
        compiler_params=pltpu.CompilerParams(vmem_limit_bytes=40 * 1024 * 1024),
    )(*args)


def route(axis, step):
    n = lax.axis_size(axis)
    return [(i, (i + step) % n) for i in range(n)]


def swap(chunks, axis):
    return lax.all_to_all(chunks, axis, 0, 0, tiled=True)


def spread(part, n):
    return jnp.broadcast_to(part[None], (n,) + part.shape)


def plane_sum(payload):
    n = lax.axis_size(PLANE)
    return jnp.sum(swap(payload.reshape(n, -1, 128), PLANE), axis=0)


def line_sum(part):
    return jnp.sum(swap(spread(part, lax.axis_size("bz")), "bz"), axis=0)


def plane_gather(part):
    return swap(spread(part, lax.axis_size(PLANE)), PLANE).reshape(-1, 128)


def local(space_factor, core_matrix, velocity_factor):
    vel_rows = velocity_factor.shape[1]
    plane = lax.axis_index(PLANE)
    count = vel_rows * lax.axis_size(PLANE)
    nz = lax.axis_size("bz")
    shape = space_factor.shape
    half = shape[2] * shape[3]
    cells = 2 * half * lax.axis_size(PLANE) * nz
    cons = jnp.asarray(constants(count))
    digit = (plane * vel_rows) // (VEL_N * VEL_N)
    v1 = SPEED_MAX * (2.0 * digit.astype(F32) + 1.0 - VEL_N) / VEL_N
    v1 = v1.reshape(1, 1)

    fa = space_factor[:, 0].reshape(RANK, half)
    fb = space_factor[:, 1].reshape(RANK, half)
    payload, tab = call(
        start_kernel, [(256, 128), (24, vel_rows)], [(408, vel_rows)], v1, velocity_factor
    )
    yl = space_factor[:, :, -1].reshape(RANK, 256)
    yh = space_factor[:, :, 0].reshape(RANK, 256)
    pad = jnp.zeros((RANK, 128 - 2 * shape[2]), F32)
    zl = jnp.concatenate([space_factor[:, :, :, -1].reshape(RANK, -1), pad], axis=1)
    zh = jnp.concatenate([space_factor[:, :, :, 0].reshape(RANK, -1), pad], axis=1)

    def halo(planes, step):
        out = []
        for field, axis in zip(planes, ("bx", "by", "bz")):
            out.append(lax.ppermute(field, axis, route(axis, step)))
        return tuple(out)

    def low_halo(*planes):
        return halo(planes, 1)

    def high_halo(*planes):
        return halo(planes, -1)

    low = low_halo(fb, yl, zl)
    high = high_halo(fa, yh, zh)
    part = plane_sum(payload)
    sums = plane_gather(part)

    def step(turn, carry):
        fa, fb, low, high, sums, rows, base, _ = carry
        kb, maps, sel, seln, gw, mode_rows, moments, civ, ginv, gain = call(
            functools.partial(maps_kernel, count, cells),
            [(RANK, half), (RANK, 464), (32, RANK), (32, RANK), (RANK, 384), (16, RANK), (8, RANK),
             (RANK, RANK), (RANK, RANK), (RANK, 16)],
            [(464, half)],
            sums, base, cons, fa, fb, high[0], low[1], high[1], low[2], high[2],
        )
        ka, yl, yh, zl, zh = call(
            plane_kernel,
            [(RANK, half), (RANK, 256), (RANK, 256), (RANK, 128), (RANK, 128)],
            [(464, half)],
            maps, sel, fa, fb, low[0], low[1], high[1], low[2], high[2], kb,
        )
        low = low_halo(kb, yl, zl)
        (part,) = call(inner_kernel, [(272, RANK)], [(272, 2 * half)], seln, ka, kb)
        (payload,) = call(edge_kernel, [(128, 128)], [], part, ka, low[0], low[1], yh, low[2], zh)
        high = high_halo(ka, yh, zh)
        sums = plane_gather(line_sum(plane_sum(payload)))
        payload, rows, base = call(
            functools.partial(core_kernel, count, cells, nz),
            [(256, 128), (RANK, vel_rows), (RANK, RANK)],
            [(408, vel_rows), (320, vel_rows)],
            v1, sums, ka, kb, rows, gain, tab, cons, gw, mode_rows, moments, civ, ginv,
            alias={4: 1},
        )
        (space,) = call(space_kernel, [shape], [], base, ka, kb)
        part = plane_sum(payload)
        part = line_sum(part)
        sums = plane_gather(part)
        return ka, kb, low, high, sums, rows, base, space

    carry = (fa, fb, low, high, sums, velocity_factor, core_matrix.T, jnp.zeros(shape, F32))
    _, _, _, _, sums, rows, base, new_space = lax.fori_loop(0, STEPS, step, carry)
    new_core, new_velocity = call(
        functools.partial(finish_kernel, count, cells),
        [(RANK, RANK), (RANK, vel_rows)], [], sums, base, rows, tab, cons,
    )
    return new_space, new_core, new_velocity


def solution(mesh):
    return jax.shard_map(
        local,
        mesh=mesh,
        in_specs=(P(None, "bx", "by", "bz"), P(), P(None, PLANE)),
        out_specs=(P(None, "bx", "by", "bz"), P(), P(None, PLANE)),
        check_vma=False,
    )
```

```python
import functools

import jax
import jax.numpy as jnp
import numpy as np
from jax import lax
from jax.experimental import pallas as pl
from jax.experimental.pallas import tpu as pltpu
from jax.sharding import PartitionSpec as P


VEL_N = 32
STEPS = 2
TIME_STEP = 0.1
SPEED_MAX = 3.0
HIGHEST = lax.Precision.HIGHEST
PLANE = ("bx", "by")
RANK = 64
F32 = jnp.float32


def mm(a, b):
    return jnp.dot(a, b, precision=HIGHEST, preferred_element_type=F32)


def mmt(a, b):
    return lax.dot_general(
        a, b, (((1,), (1,)), ((), ())), precision=HIGHEST, preferred_element_type=F32
    )


def np_tables(row_total):
    row_ids = np.arange(row_total)
    levels = np.stack([row_ids // (VEL_N * VEL_N), row_ids // VEL_N % VEL_N, row_ids % VEL_N])
    v = SPEED_MAX * (2.0 * levels + 1.0 - VEL_N) / VEL_N
    w = np.exp(-0.5 * np.sum(v * v, axis=0)) / line_mean() ** 3
    modes = np.stack(
        [w, w * v[0], w * v[1], w * v[2]]
        + [0.5 * w * (v[d] * v[d] - 1.0) for d in range(3)]
        + [w * v[0] * v[1], w * v[0] * v[2], w * v[1] * v[2]]
    )
    weights = [np.ones_like(w)]
    for d in range(3):
        weights += [np.maximum(v[d], 0.0), np.minimum(v[d], 0.0)]
    return v, modes, np.stack(weights)


def line_mean():
    line = SPEED_MAX * (2.0 * np.arange(VEL_N) + 1.0 - VEL_N) / VEL_N
    return float(np.mean(np.exp(-0.5 * line * line)))


def constants(row_total):
    v, modes, weights = np_tables(row_total)
    gram = np.einsum("wv,mv,nv->wmn", weights, modes, modes)
    out = np.zeros((160, 16), np.float32)
    for w in range(7):
        out[16 * w : 16 * w + 10, :10] = gram[w]
    out[112, :10] = modes.sum(axis=1)
    for d in range(3):
        out[113 + d, :10] = modes @ v[d]
    first = [0, 1, 2, 3, 1, 2, 3, 1, 1, 2]
    second = [None, None, None, None, 1, 2, 3, 2, 3, 3]
    for r in range(10):
        out[120 + r, first[r]] = 1.0
        if second[r] is not None:
            out[136 + r, second[r]] = 1.0
    return out


def iota(shape, dim):
    return lax.broadcasted_iota(jnp.int32, shape, dim)


def eye():
    return (iota((RANK, RANK), 0) == iota((RANK, RANK), 1)).astype(F32)


def spread_lane(block, k):
    return jnp.broadcast_to(block[:, k : k + 1], (8, 128))


def spread_row(block, r):
    return jnp.broadcast_to(block[r : r + 1, :], (8, 128))


def chol_inverse(gram, width=4):
    lane = iota((8, 128), 1)
    sub = iota((8, 128), 0)
    on_diag = gram * eye()
    diag = jnp.sum(on_diag, axis=0, keepdims=True)
    row_scale = lax.rsqrt(diag)
    scaled = gram * row_scale * lax.rsqrt(jnp.sum(on_diag, axis=1, keepdims=True))
    wide = jnp.concatenate([scaled, jnp.zeros_like(gram)], axis=1)
    blocks = []
    for b in range(8):
        unit = jnp.where(lane == sub + (64 + 8 * b), 1.0, 0.0)
        blocks.append(wide[8 * b : 8 * b + 8] + unit)
    for k in range(0, RANK, width):
        b, r = divmod(k, 8)
        left = range(b, 8)
        cols = [{i: spread_lane(blocks[i], k + j) for i in left} for j in range(width)]
        heads = [spread_row(blocks[b], r + j) for j in range(width)]
        for j in range(0, width, 2):
            p = spread_row(cols[j][b], r + j)
            q = spread_row(cols[j][b], r + j + 1)
            s = spread_row(cols[j + 1][b], r + j + 1)
            inv_p = lax.rsqrt(p)
            both = inv_p * lax.rsqrt(p * s - q * q)
            pb, qb = both * p, both * q
            for i in left:
                first = cols[j][i]
                cols[j][i] = first * inv_p
                cols[j + 1][i] = pb * cols[j + 1][i] - qb * first
            first = heads[j]
            heads[j] = first * inv_p
            heads[j + 1] = pb * heads[j + 1] - qb * first
            for m in range(j + 2, width):
                u = spread_row(cols[j][b], r + m)
                w = spread_row(cols[j + 1][b], r + m)
                for i in left:
                    cols[m][i] = (cols[m][i] - cols[j][i] * u) - cols[j + 1][i] * w
                heads[m] = (heads[m] - heads[j] * u) - heads[j + 1] * w
        for i in left:
            if i == b and r + width == 8:
                new = blocks[i]
            else:
                new = blocks[i]
                for j in range(width):
                    new = new - cols[j][i] * heads[j]
            if i == b:
                new = jnp.where(sub >= r + width, new, blocks[i])
                for j in range(width):
                    new = jnp.where(sub == r + j, heads[j], new)
            blocks[i] = new
    full = jnp.concatenate(blocks, axis=0)
    keep = iota((RANK, RANK), 1) >= iota((RANK, RANK), 0)
    upper = jnp.where(keep, full[:, :RANK], 0.0) * (diag * row_scale)
    return upper, full[:, RANK:] * row_scale


def features(sel_map, field):
    both = mm(sel_map, field)
    lift = jnp.where(iota((16, field.shape[1]), 0) < 4, 1.0, 0.0)
    return both[:16] * (both[16:] + lift)


def pair_block(plus, minus):
    return jnp.where(iota((RANK, RANK), 0) <= iota((RANK, RANK), 1), plus, minus)


def weighted_payload(rows, v1, tab_ref, out_ref, stack_ref, scale, collide):
    modes = tab_ref[0:16, :]
    v2, v3 = tab_ref[18:19, :], tab_ref[19:20, :]
    weights = [None, jnp.maximum(v2, 0.0), jnp.minimum(v2, 0.0)]
    weights += [jnp.maximum(v3, 0.0), jnp.minimum(v3, 0.0)]
    for i in range(5):
        w = weights[i]
        stack_ref[80 * i : 80 * i + 64, :] = rows if w is None else rows * w
        stack_ref[80 * i + 64 : 80 * i + 80, :] = modes if w is None else modes * w
    stack_ref[400:408, :] = tab_ref[16:24, :]
    res = mmt(stack_ref[...], rows) * scale
    quads = [res[80 * i : 80 * i + 64] for i in range(5)]
    cross = [res[80 * i + 64 : 80 * i + 80] for i in range(5)]
    out_ref[...] = jnp.zeros_like(out_ref)
    out_ref[0:64, 0:64] = quads[0]
    out_ref[128:144, 0:64] = cross[0]
    if collide is not None:
        out_ref[136:152, 64:128] = collide
    v1p, v1m = jnp.maximum(v1, 0.0), jnp.minimum(v1, 0.0)
    pairs = [(quads[0] * v1p, quads[0] * v1m), (quads[1], quads[2]), (quads[3], quads[4])]
    crosses = [cross[0] * v1p, cross[0] * v1m] + cross[1:]
    out_ref[0:64, 64:128] = pair_block(*pairs[1])
    out_ref[64:128, 0:64] = pair_block(*pairs[0])
    out_ref[64:128, 64:128] = pair_block(*pairs[2])
    for i in range(6):
        out_ref[144 + 16 * i : 160 + 16 * i, 0:64] = crosses[i]
    out_ref[128:136, 64:128] = res[400:408]
    for d in range(3):
        diag = jnp.sum(pairs[d][1] * eye(), axis=0, keepdims=True)
        out_ref[152 + d : 153 + d, 64:128] = diag


def start_kernel(v1_ref, rows_ref, out_ref, tab_ref, stack_ref):
    v1 = v1_ref[0, 0]
    lanes = tab_ref.shape[1]
    at = iota((1, lanes), 1)
    v2 = SPEED_MAX * (2.0 * (at // VEL_N).astype(F32) + 1.0 - VEL_N) / VEL_N
    v3 = SPEED_MAX * (2.0 * (at % VEL_N).astype(F32) + 1.0 - VEL_N) / VEL_N
    v1 = jnp.full((1, lanes), v1, F32)
    w = jnp.exp(-0.5 * (v1 * v1 + v2 * v2 + v3 * v3)) / (line_mean() ** 3)
    tab_ref[...] = jnp.zeros_like(tab_ref)
    modes = [w, w * v1, w * v2, w * v3]
    modes += [0.5 * w * (v * v - 1.0) for v in (v1, v2, v3)]
    modes += [w * v1 * v2, w * v1 * v3, w * v2 * v3]
    for i, m in enumerate(modes):
        tab_ref[i : i + 1, :] = m
    for i, m in enumerate([jnp.ones_like(v1), v1, v2, v3]):
        tab_ref[16 + i : 17 + i, :] = m
    weighted_payload(rows_ref[...], v1_ref[0, 0], tab_ref, out_ref, stack_ref, 1.0, None)


def symmetric(sums, gain, cons):
    upper = iota((RANK, RANK), 0) <= iota((RANK, RANK), 1)
    diag = iota((RANK, RANK), 0) == iota((RANK, RANK), 1)
    packs = [sums[64:128, 0:64], sums[0:64, 64:128], sums[64:128, 64:128]]
    grams = [sums[0:64, 0:64]]
    for d in range(3):
        turned = packs[d].T
        grams.append(jnp.where(upper, packs[d], turned))
        grams.append(
            jnp.where(diag, sums[152 + d : 153 + d, 64:128], jnp.where(upper, turned, packs[d]))
        )
    mode_gain = mmt(cons[0:120], gain)
    for w in range(7):
        half = sums[128 + 16 * w : 144 + 16 * w, 0:64] + 0.5 * mode_gain[16 * w : 16 * w + 16]
        cross = mm(gain, half)
        grams[w] = grams[w] + (cross + cross.T)
    mode_rows = sums[128:144, 0:64] + mode_gain[0:16]
    moments = sums[128:136, 64:128] + mode_gain[112:120]
    return grams, mode_rows, moments


def shifted_stack(p, stack_ref, mine, lower, upper, yl_ref, yh_ref, zl_ref, zh_ref):
    lane = iota((RANK, 128), 1)
    field = mine[...]
    stack_ref[0:64, :] = field
    stack_ref[64:128, :] = lower[...]
    stack_ref[256:320, :] = upper[...]
    n = field.shape[1] // 128
    zl, zh = zl_ref[...], zh_ref[...]
    for y in range(n):
        here = field[:, 128 * y : 128 * y + 128]
        cols = slice(128 * y, 128 * y + 128)
        halo = slice(128 * p, 128 * p + 128)
        stack_ref[128:192, cols] = yl_ref[:, halo] if y == 0 else field[:, 128 * (y - 1) : 128 * y]
        stack_ref[320:384, cols] = (
            yh_ref[:, halo] if y == n - 1 else field[:, 128 * (y + 1) : 128 * (y + 2)]
        )
        g = p * n + y
        low = pltpu.roll(zl, (128 - g) % 128, 1)
        stack_ref[192:256, cols] = jnp.where(lane == 0, low, pltpu.roll(here, 1, 1))
        high = pltpu.roll(zh, 127 - g, 1)
        stack_ref[384:448, cols] = jnp.where(lane == 127, high, pltpu.roll(here, 127, 1))


def columns(fields, lane_at):
    lane = iota((RANK, 128), 1)
    out = jnp.zeros((RANK, 128), F32)
    g = 0
    for field in fields:
        for y in range(field.shape[1] // 128):
            here = field[:, 128 * y : 128 * y + 128]
            out = jnp.where(lane == g, pltpu.roll(here, (g - lane_at) % 128, 1), out)
            g += 1
    return out


def maps_kernel(
    count, cells, sums_ref, base_ref, cons_ref, fa, fb, xl, xh, yl, yh, zl, zh,
    kb_ref, ka_ref, ylo_ref, yho_ref, zlo_ref, zho_ref,
    seln_ref, gw_ref, mode_ref, mom_ref, civ_ref, ginv_ref, gain_ref, stack_ref, other_ref,
):
    sums, base, cons = sums_ref[...], base_ref[...], cons_ref[...]
    gain = (TIME_STEP / cells) * mmt(base, sums[136:152, 64:128])
    gain_ref[...] = gain
    grams, mode_rows, moments = symmetric(sums, gain, cons)
    shifted_stack(1, stack_ref, fb, fa, xh, yl, yh, zl, zh)
    shifted_stack(0, other_ref, fa, xl, fb, yl, yh, zl, zh)
    sides = mm(jnp.concatenate(grams, axis=0), base)
    sides = [sides[64 * w : 64 * w + 64] for w in range(7)]
    stay = (1.0 - TIME_STEP) * sides[0]
    for d in range(3):
        stay = stay + TIME_STEP * (sides[2 * d + 2] - sides[2 * d + 1])
    row = [stay] + [TIME_STEP * sides[2 * d + 1] for d in range(3)]
    row += [-TIME_STEP * sides[2 * d + 2] for d in range(3)] + [TIME_STEP * mode_rows.T]
    row = jnp.concatenate(row, axis=1) * (1.0 / count)
    sel = mm(cons[120:152, 0:8], mm(moments, base) * (1.0 / count))
    stack_ref[448:464, :] = features(sel, fb[...])
    other_ref[448:464, :] = features(sel, fa[...])
    gw_ref[...] = jnp.concatenate(grams[1:], axis=1)
    mode_ref[...] = mode_rows
    mom_ref[...] = moments
    _, civ = chol_inverse(grams[0] * (1.0 / count))
    maps = mm(civ, row)
    kb = mm(maps, stack_ref[...])
    ka = mm(maps, other_ref[...])
    kb_ref[...] = kb
    ka_ref[...] = ka
    n = ka.shape[1]
    ylo_ref[...] = jnp.concatenate([ka[:, n - 128 :], kb[:, n - 128 :]], axis=1)
    yho_ref[...] = jnp.concatenate([ka[:, :128], kb[:, :128]], axis=1)
    zlo_ref[...] = columns((ka, kb), 127)
    zho_ref[...] = columns((ka, kb), 0)
    civ_ref[...] = civ
    ginv_ref[...] = mm(civ.T, civ) * (1.0 / count)
    seln_ref[...] = mm(cons[120:152, 0:8], mmt(moments, civ) * (1.0 / count))


def inner_kernel(seln_ref, ka, kb, out_ref, stack_ref):
    lane = iota((RANK, 128), 1)
    n = ka.shape[1]
    zero = jnp.zeros((RANK, 128), F32)
    for p, ref in enumerate((ka, kb)):
        at = p * n
        field = ref[...]
        stack_ref[0:64, at : at + n] = field
        stack_ref[128:192, at : at + 128] = zero
        stack_ref[128:192, at + 128 : at + n] = field[:, : n - 128]
        for y in range(n // 128):
            here = field[:, 128 * y : 128 * y + 128]
            stack_ref[192:256, at + 128 * y : at + 128 * y + 128] = jnp.where(
                lane == 0, 0.0, pltpu.roll(here, 1, 1)
            )
        stack_ref[256:272, at : at + n] = features(seln_ref[...], field)
    stack_ref[64:128, 0:n] = jnp.zeros((RANK, n), F32)
    stack_ref[64:128, n : 2 * n] = ka[...]
    out_ref[...] = mmt(stack_ref[...], stack_ref[0:64, :])


def edge_kernel(part_ref, ka, xl, yl, yh, zl, zh, out_ref):
    part = part_ref[...]
    out_ref[0:64, 0:64] = part[0:64]
    out_ref[32:48, 0:32] = part[256:272, 0:32]
    out_ref[48:64, 0:32] = part[256:272, 32:64]
    out_ref[0:64, 64:128] = part[64:128] + mmt(xl[...], ka[...])
    out_ref[64:128, 0:64] = part[128:192] + mmt(yl[...], yh[...])
    out_ref[64:128, 64:128] = part[192:256] + mmt(zl[...], zh[...])


def core_kernel(
    count, cells, nz, v1_ref, sums_ref, ka, kb, rows_ref, gain_ref, tab_ref, cons_ref,
    gw_ref, mode_ref, mom_ref, civ_ref, ginv_ref, out_ref, rows_out, cxi_ref, stack_ref, base_ref,
):
    v1 = v1_ref[0, 0]
    rows = rows_ref[...] + mm(gain_ref[...], tab_ref[0:16, :])
    v2, v3 = tab_ref[18:19, :], tab_ref[19:20, :]
    base_ref[0:64, :] = rows
    base_ref[64:128, :] = rows * jnp.maximum(v2, 0.0)
    base_ref[128:192, :] = rows * jnp.minimum(v2, 0.0)
    base_ref[192:256, :] = rows * jnp.maximum(v3, 0.0)
    base_ref[256:320, :] = rows * jnp.minimum(v3, 0.0)
    sums = sums_ref[...] * (1.0 / cells)
    civ = civ_ref[...]
    unit = eye()
    gram = sums[0:64, 0:64]
    corner = (iota((RANK, RANK), 0) >= 32) & (iota((RANK, RANK), 1) < 32)
    up, cxi = chol_inverse(jnp.where(corner, gram.T, gram))
    cxi_ref[...] = cxi
    moment_x = jnp.concatenate([sums[32:48, 0:32], sums[48:64, 0:32]], axis=1)
    y = mm(up, civ)
    zs = jnp.concatenate([sums[0:64, 64:128], sums[64:128, 0:64], sums[64:128, 64:128]], axis=0)
    zs = mmt(zs, cxi)
    lower, upper = [], []
    for d in range(3):
        turned = mm(cxi, zs[64 * d : 64 * d + 64])
        lower.append(unit - turned.T)
        upper.append(turned - unit)
    yg = mm(y, gw_ref[...])
    yg = jnp.concatenate([yg[:, 64 * w : 64 * w + 64] for w in range(6)], axis=0)
    sides = jnp.concatenate([lower[0], upper[0], lower[1], upper[1], lower[2], upper[2]], axis=1)
    rate = mm(mmt(cxi, moment_x), mode_ref[...]) - mm(sides, yg)
    y = (1.0 + TIME_STEP) * y - TIME_STEP * mm(rate, ginv_ref[...])
    sel = mm(cons_ref[120:152, 0:8], mm(mmt(mom_ref[...], y) * (1.0 / count), cxi))
    collide = mmt(features(sel, ka[...]), ka[...]) + mmt(features(sel, kb[...]), kb[...])
    turn = lower[0] * jnp.maximum(v1, 0.0) + upper[0] * jnp.minimum(v1, 0.0)
    move = [(1.0 - TIME_STEP) * unit - TIME_STEP * turn]
    move += [-TIME_STEP * m for m in (lower[1], upper[1], lower[2], upper[2])]
    move = mm(jnp.concatenate(move, axis=0), y)
    move = jnp.concatenate([move[64 * t : 64 * t + 64] for t in range(5)], axis=1)
    rows = mm(move, base_ref[...])
    rows_out[...] = rows
    weighted_payload(rows, v1, tab_ref, out_ref, stack_ref, 1.0 / nz, collide)


def space_kernel(cxi_ref, ka, kb, out_ref):
    for p, ref in enumerate((ka, kb)):
        field = mm(cxi_ref[...], ref[...])
        for y in range(out_ref.shape[2]):
            out_ref[:, p, y, :] = field[:, 128 * y : 128 * y + 128]


def finish_kernel(count, cells, sums_ref, cxi_ref, rows_ref, tab_ref, cons_ref, low_ref, out_ref):
    sums = sums_ref[...]
    gain = (TIME_STEP / cells) * mmt(cxi_ref[...], sums[136:152, 64:128])
    half = sums[128:144, 0:64] + 0.5 * mmt(cons_ref[0:16, :], gain)
    cross = mm(gain, half)
    up, civ = chol_inverse((sums[0:64, 0:64] + (cross + cross.T)) * (1.0 / count))
    low_ref[...] = up.T
    out_ref[...] = mm(civ, rows_ref[...] + mm(gain, tab_ref[0:16, :]))


def call(kernel, outs, scratch, *args, alias=None):
    shapes = [jax.ShapeDtypeStruct(s, F32) for s in outs]
    specs = [pl.BlockSpec(memory_space=pltpu.VMEM) for _ in args]
    if args[0].shape == (1, 1):
        specs[0] = pl.BlockSpec(memory_space=pltpu.SMEM)
    return pl.pallas_call(
        kernel,
        out_shape=shapes,
        in_specs=specs,
        out_specs=[pl.BlockSpec(memory_space=pltpu.VMEM) for _ in outs],
        scratch_shapes=[pltpu.VMEM(s, F32) for s in scratch],
        input_output_aliases=alias or {},
        compiler_params=pltpu.CompilerParams(vmem_limit_bytes=40 * 1024 * 1024),
    )(*args)


def route(axis, step):
    n = lax.axis_size(axis)
    return [(i, (i + step) % n) for i in range(n)]


def swap(chunks, axis):
    return lax.all_to_all(chunks, axis, 0, 0, tiled=True)


def spread(part, n):
    return jnp.broadcast_to(part[None], (n,) + part.shape)


def plane_sum(payload):
    n = lax.axis_size(PLANE)
    return jnp.sum(swap(payload.reshape(n, -1, 128), PLANE), axis=0)


def line_sum(part):
    return jnp.sum(swap(spread(part, lax.axis_size("bz")), "bz"), axis=0)


def plane_gather(part):
    return swap(spread(part, lax.axis_size(PLANE)), PLANE).reshape(-1, 128)


def local(space_factor, core_matrix, velocity_factor):
    vel_rows = velocity_factor.shape[1]
    plane = lax.axis_index(PLANE)
    count = vel_rows * lax.axis_size(PLANE)
    nz = lax.axis_size("bz")
    shape = space_factor.shape
    half = shape[2] * shape[3]
    cells = 2 * half * lax.axis_size(PLANE) * nz
    cons = jnp.asarray(constants(count))
    digit = (plane * vel_rows) // (VEL_N * VEL_N)
    v1 = SPEED_MAX * (2.0 * digit.astype(F32) + 1.0 - VEL_N) / VEL_N
    v1 = v1.reshape(1, 1)

    fa = space_factor[:, 0].reshape(RANK, half)
    fb = space_factor[:, 1].reshape(RANK, half)
    payload, tab = call(
        start_kernel, [(256, 128), (24, vel_rows)], [(408, vel_rows)], v1, velocity_factor
    )
    yl = space_factor[:, :, -1].reshape(RANK, 256)
    yh = space_factor[:, :, 0].reshape(RANK, 256)
    pad = jnp.zeros((RANK, 128 - 2 * shape[2]), F32)
    zl = jnp.concatenate([space_factor[:, :, :, -1].reshape(RANK, -1), pad], axis=1)
    zh = jnp.concatenate([space_factor[:, :, :, 0].reshape(RANK, -1), pad], axis=1)

    def halo(planes, step):
        out = []
        for field, axis in zip(planes, ("bx", "by", "bz")):
            out.append(lax.ppermute(field, axis, route(axis, step)))
        return tuple(out)

    def low_halo(*planes):
        return halo(planes, 1)

    def high_halo(*planes):
        return halo(planes, -1)

    low = low_halo(fb, yl, zl)
    high = high_halo(fa, yh, zh)
    part = plane_sum(payload)
    sums = plane_gather(part)

    def step(turn, carry):
        fa, fb, low, high, sums, rows, base, _ = carry
        kb, ka, yl, yh, zl, zh, seln, gw, mode_rows, moments, civ, ginv, gain = call(
            functools.partial(maps_kernel, count, cells),
            [(RANK, half), (RANK, half), (RANK, 256), (RANK, 256), (RANK, 128), (RANK, 128),
             (32, RANK), (RANK, 384), (16, RANK), (8, RANK), (RANK, RANK), (RANK, RANK), (RANK, 16)],
            [(464, half), (464, half)],
            sums, base, cons, fa, fb, low[0], high[0], low[1], high[1], low[2], high[2],
        )
        low = low_halo(kb, yl, zl)
        (part,) = call(inner_kernel, [(272, RANK)], [(272, 2 * half)], seln, ka, kb)
        (payload,) = call(edge_kernel, [(128, 128)], [], part, ka, low[0], low[1], yh, low[2], zh)
        high = high_halo(ka, yh, zh)
        sums = plane_gather(line_sum(plane_sum(payload)))
        payload, rows, base = call(
            functools.partial(core_kernel, count, cells, nz),
            [(256, 128), (RANK, vel_rows), (RANK, RANK)],
            [(408, vel_rows), (320, vel_rows)],
            v1, sums, ka, kb, rows, gain, tab, cons, gw, mode_rows, moments, civ, ginv,
            alias={4: 1},
        )
        (space,) = call(space_kernel, [shape], [], base, ka, kb)
        part = plane_sum(payload)
        part = line_sum(part)
        sums = plane_gather(part)
        return ka, kb, low, high, sums, rows, base, space

    carry = (fa, fb, low, high, sums, velocity_factor, core_matrix.T, jnp.zeros(shape, F32))
    _, _, _, _, sums, rows, base, new_space = lax.fori_loop(0, STEPS, step, carry)
    new_core, new_velocity = call(
        functools.partial(finish_kernel, count, cells),
        [(RANK, RANK), (RANK, vel_rows)], [], sums, base, rows, tab, cons,
    )
    return new_space, new_core, new_velocity


def solution(mesh):
    return jax.shard_map(
        local,
        mesh=mesh,
        in_specs=(P(None, "bx", "by", "bz"), P(), P(None, PLANE)),
        out_specs=(P(None, "bx", "by", "bz"), P(), P(None, PLANE)),
        check_vma=False,
    )
```
